32 devices in a mesh: ctx: 8 (over y, x, core), tp: 4 (over z).
Axes of the slice: x: 2, y: 2, z: 4, core: 2. Of those that a mesh axis runs over, the one named last changes fastest.
Arguments:
- inputs: bfloat16 [4096, 2048], P(('ctx', 'tp')), may hold values from -54 to 54
- norm_gain: float32 [2048], replicated, may hold values from 0.1 to 1.9
- qkv_weight: bfloat16 [2048, 3, 2048], P(None, None, 'tp'), may hold values from -0.125 to 0.125
- head_gain: float32 [2048], P('tp'), may hold values from 0.1 to 1.9
- out_weight: bfloat16 [2048, 2048], P('tp'), may hold values from -0.125 to 0.125
- out_cotangent: bfloat16 [4096, 2048], P(('ctx', 'tp')), may hold values from -6 to 6
Outputs:
- outputs: bfloat16 [4096, 2048], P(('ctx', 'tp'))
- input_grad: bfloat16 [4096, 2048], P(('ctx', 'tp'))
- qkv_grad: float32 [2048, 3, 2048], P('ctx', None, 'tp')
- out_grad_t: float32 [2048, 2048], P('ctx', 'tp')
The draws below stay inside these ranges and needn't reach their ends.
All inputs are finite; a program needn't handle non-finite values.
Results may differ from the reference program's by a relative error of at most 0.015.
The reference program's roundings to bfloat16 on the way (of `normed`, `projected`, `scores`, `mixed`, `grad_attended`, `grad_scores` and `grad_proj`) count: a program that leaves them out, or rounds other values in their place, can miss the bound.
Values may be sent and summed in bfloat16 or wider, within the bound.
A program may use at most 128 MiB of HBM per device.

```python
import math
import jax
import jax.numpy as jnp
from jax import lax

D = 2048
H = 16
DH = 128
GROUP = 512
TOKENS = 4096


def draw_inputs(key, part):
    base_key, row_key, column_key = jax.random.split(key, 3)
    base = jax.random.truncated_normal(base_key, -6.0, 6.0, (TOKENS, D), jnp.float32)
    row_scales = jnp.exp(jax.random.uniform(row_key, (TOKENS, 1), jnp.float32, math.log(0.3), math.log(3.0)))
    column_scales = jnp.exp(jax.random.uniform(column_key, (1, D), jnp.float32, math.log(0.3), math.log(3.0)))
    return (base * row_scales * column_scales).astype(jnp.bfloat16)


def spiked(drawn, stream_key, source, target, blocks, factor):
    def block_of(dim):
        return (jnp.arange(drawn.shape[dim]) // (drawn.shape[dim] // blocks)).reshape((-1,) + (1,) * (drawn.ndim - 1 - dim))

    near = jax.random.permutation(stream_key, blocks)[block_of(target)]
    second = (block_of(target) + blocks // 2) % blocks
    return jnp.where((block_of(source) == near) | (block_of(source) == second), factor * drawn, drawn)


def level_of(rng, dims, shards, low, high):
    loudness = 1.0
    for position, blocks in shards:
        heights = jax.random.uniform(jax.random.fold_in(jax.random.fold_in(rng, 6), position), (blocks,), jnp.float32, low / len(shards), high / len(shards))
        loudness = loudness * jnp.repeat(jnp.exp(heights), dims[position] // blocks).reshape((-1,) + (1,) * (len(dims) - 1 - position))
    return loudness


def gaussian(stream_key, shape, deviation, limit, shards=(), dtype=jnp.bfloat16):
    result = jax.random.normal(stream_key, shape, jnp.float32) * deviation
    if len(shards) > 0:
        result = level_of(stream_key, shape, shards, -0.22, 0.18) * result
    return jnp.clip(result, min=-limit, max=limit).astype(dtype)


def bell_draw_with(stream_key, extent, scale, most, pieces, heavy, held_as=jnp.bfloat16):
    result = scale * jax.random.normal(stream_key, extent, jnp.float32)
    if pieces:
        result = result * level_of(stream_key, extent, pieces, -0.22, 0.18)
    return jnp.clip(spiked(result, jax.random.fold_in(stream_key, 3), *heavy), -most, most).astype(held_as)


def setup_inputs(seed: int = 0) -> dict:
    keys = jax.random.split(jax.random.key(seed), 7)
    inputs = draw_inputs(jax.random.fold_in(keys[6], 71), 0)
    norm_gain = jnp.clip(1.0 + 0.18 * jax.random.normal(keys[1], (D,), jnp.float32), 0.1, 1.9)
    qkv_weight = gaussian(keys[2], (D, 3, D), D ** -0.5, 0.125, ((2, 4),))
    head_gain = jnp.clip(1.0 + 0.18 * jax.random.normal(keys[3], (D,), jnp.float32), 0.1, 1.9)
    out_weight = gaussian(keys[4], (D, D), D ** -0.5, 0.125, ((0, 4),))
    out_cotangent = bell_draw_with(keys[5], (TOKENS, D), 1.0, 6.0, ((0, 32),), (0, 1, 32, 2.75))
    return {"inputs": inputs, "norm_gain": norm_gain, "qkv_weight": qkv_weight, "head_gain": head_gain, "out_weight": out_weight, "out_cotangent": out_cotangent}


EPSILON = 1e-05
highest = lax.Precision.HIGHEST

def row_scale(rows):
    return lax.rsqrt(lax.optimization_barrier(jnp.mean(rows * rows, axis=-1, keepdims=True)) + EPSILON)

def rounded(value):
    return lax.optimization_barrier(value.astype(jnp.bfloat16))

def masked_scores(query, key_block):
    causal = jnp.arange(GROUP)[:, None] >= jnp.arange(GROUP)[None, :]
    raw = jnp.einsum('thd,shd->hts', query, key_block, precision=highest)
    return rounded(jnp.where(causal[None], raw, 0.0)).astype(jnp.float32)

def reference(inputs, norm_gain, qkv_weight, head_gain, out_weight, out_cotangent):
    tokens_all = inputs.shape[0]
    width = inputs.shape[1]
    blocks = tokens_all // GROUP
    factor = 1.0 / math.sqrt(TOKENS)
    inputs_f = inputs.astype(jnp.float32)
    scale_in = row_scale(inputs_f)
    normed = rounded(inputs_f * scale_in * norm_gain)
    flat_weight = qkv_weight.reshape(width, 3 * width)
    projected = rounded(jnp.dot(normed, flat_weight, preferred_element_type=jnp.float32))
    split_parts = projected.reshape(blocks, GROUP, 3, H, DH).astype(jnp.float32)
    queries = split_parts[:, :, 0]
    key_rows = split_parts[:, :, 1]
    values = split_parts[:, :, 2]
    block_states = jnp.einsum('bshd,bshe->bhde', key_rows, values, precision=highest)
    zero_state = jnp.zeros_like(block_states[:1])
    states = jnp.concatenate([zero_state, jnp.cumsum(block_states, axis=0)[:-1]], axis=0)

    def forward_block(item):
        query, key_block, value, state = item
        scores = masked_scores(query, key_block)
        local_part = jnp.einsum('hts,she->the', scores, value, precision=highest)
        carried = jnp.einsum('thd,hde->the', query, state, precision=highest)
        return local_part + carried
    attended = lax.map(forward_block, (queries, key_rows, values, states))
    scale_head = row_scale(attended)
    gains = head_gain.reshape(H, DH)
    mixed = rounded(attended * scale_head * gains).reshape(tokens_all, width)
    outputs = (inputs_f + jnp.dot(mixed, out_weight, preferred_element_type=jnp.float32)).astype(jnp.bfloat16)
    grad_mixed = jnp.dot(out_cotangent, out_weight.T, preferred_element_type=jnp.float32).reshape(blocks, GROUP, H, DH)
    weighted = grad_mixed * gains
    cube_head = scale_head * scale_head * scale_head
    grad_attended = rounded(scale_head * weighted - cube_head * attended * lax.optimization_barrier(jnp.mean(weighted * attended, axis=-1, keepdims=True))).astype(jnp.float32)
    grad_blocks = jnp.einsum('bthd,bthe->bhde', queries, grad_attended, precision=highest)
    reversed_sums = jnp.cumsum(grad_blocks[::-1], axis=0)[::-1]
    grad_states = jnp.concatenate([reversed_sums[1:], zero_state], axis=0)

    def backward_block(item):
        query, key_block, value, grad_part, state, grad_state = item
        causal = jnp.arange(GROUP)[:, None] >= jnp.arange(GROUP)[None, :]
        scores = masked_scores(query, key_block)
        raw = jnp.einsum('the,she->hts', grad_part, value, precision=highest)
        grad_scores = rounded(jnp.where(causal[None], raw, 0.0)).astype(jnp.float32)
        grad_query = jnp.einsum('hts,shd->thd', grad_scores, key_block, precision=highest) + jnp.einsum('the,hde->thd', grad_part, state, precision=highest)
        grad_key = jnp.einsum('hts,thd->shd', grad_scores, query, precision=highest) + jnp.einsum('she,hde->shd', value, grad_state, precision=highest)
        grad_value = jnp.einsum('hts,the->she', scores, grad_part, precision=highest) + jnp.einsum('shd,hde->she', key_block, grad_state, precision=highest)
        return jnp.stack([grad_query, grad_key, grad_value], axis=1)
    grad_all = lax.map(backward_block, (queries, key_rows, values, grad_attended, states, grad_states))
    grad_proj = rounded(grad_all).reshape(tokens_all, 3 * width)
    grad_normed = jnp.dot(grad_proj, flat_weight.T, preferred_element_type=jnp.float32)
    weighted_in = grad_normed * norm_gain
    cube_in = scale_in * scale_in * scale_in
    input_grad = (out_cotangent.astype(jnp.float32) + scale_in * weighted_in - cube_in * inputs_f * lax.optimization_barrier(jnp.mean(weighted_in * inputs_f, axis=-1, keepdims=True))).astype(jnp.bfloat16)
    qkv_grad = jnp.dot(normed.T, grad_proj, preferred_element_type=jnp.float32).reshape(width, 3, width) * factor
    out_grad_t = jnp.dot(out_cotangent.T, mixed, preferred_element_type=jnp.float32) * factor
    return (outputs, input_grad, qkv_grad, out_grad_t)
```

```python
import functools
import math

import jax
import jax.numpy as jnp
from jax import lax
from jax.experimental import pallas as pl
from jax.experimental.pallas import tpu as pltpu
from jax.sharding import PartitionSpec as P

DH = 128
EPSILON = 1e-05
MESH = pl.DeviceIdType.MESH
F32 = jnp.float32
BF16 = jnp.bfloat16
VMEM_LIMIT = 60 * 1024 * 1024
NN = (((1,), (0,)), ((), ()))
NT = (((1,), (1,)), ((), ()))
TN = (((0,), (0,)), ((), ()))


def dot(a, b, dims=NN):
    return lax.dot_general(a, b, dims, preferred_element_type=F32)


def row_scale(rows):
    return lax.rsqrt(jnp.mean(rows * rows, axis=-1, keepdims=True) + EPSILON)


def split(value):
    high = value.astype(BF16)
    return high, (value - high.astype(F32)).astype(BF16)


def line_barrier(ctx, me, n, others):
    barrier = pltpu.get_barrier_semaphore()

    @pl.when(me > 0)
    def _():
        pl.semaphore_signal(barrier, inc=1, device_id=(ctx, me - 1), device_id_type=MESH)

    @pl.when(me < n - 1)
    def _():
        pl.semaphore_signal(barrier, inc=1, device_id=(ctx, me + 1), device_id_type=MESH)

    for other in others:
        pl.semaphore_signal(barrier, inc=1, device_id=(other, me), device_id_type=MESH)
    inner = jnp.logical_and(me > 0, me < n - 1)

    @pl.when(inner)
    def _():
        pl.semaphore_wait(barrier, 2 + len(others))

    @pl.when(jnp.logical_not(inner))
    def _():
        pl.semaphore_wait(barrier, 1 + len(others))


class LineGather:
    def __init__(self, ctx, me, n, own, held, send, recv):
        self.ctx, self.me, self.n = ctx, me, n
        self.own, self.held, self.send, self.recv = own, held, send, recv

    def copy(self, source, origin, up):
        target = self.me + 1 if up else self.me - 1
        return pltpu.make_async_remote_copy(
            src_ref=source,
            dst_ref=self.held.at[origin],
            send_sem=self.send.at[1 if up else 0, origin],
            recv_sem=self.recv.at[origin],
            device_id=(self.ctx, target),
            device_id_type=MESH,
        )

    def start(self):
        @pl.when(self.me < self.n - 1)
        def _():
            self.copy(self.own, self.me, True).start()

        @pl.when(self.me > 0)
        def _():
            self.copy(self.own, self.me, False).start()

    def step(self, d):
        below, above = self.me - d, self.me + d

        @pl.when(below >= 0)
        def _():
            self.copy(self.held.at[below], below, True).wait_recv()

            @pl.when(self.me < self.n - 1)
            def _():
                self.copy(self.held.at[below], below, True).start()

        @pl.when(above < self.n)
        def _():
            self.copy(self.held.at[above], above, False).wait_recv()

            @pl.when(self.me > 0)
            def _():
                self.copy(self.held.at[above], above, False).start()

    def finish(self):
        for origin in range(self.n):

            @pl.when(jnp.logical_and(origin <= self.me, self.me < self.n - 1))
            def _():
                self.copy(self.held.at[origin], origin, True).wait_send()

            @pl.when(jnp.logical_and(origin >= self.me, self.me > 0))
            def _():
                self.copy(self.held.at[origin], origin, False).wait_send()


class LineScatter:
    def __init__(self, ctx, me, n, partial, total, out, up_in, down_in, send, recv):
        self.ctx, self.me, self.n = ctx, me, n
        self.partial, self.total, self.out = partial, total, out
        self.arrived = (down_in, up_in)
        self.send, self.recv = send, recv

    def copy(self, t, up):
        target = self.me + 1 if up else self.me - 1
        side = 1 if up else 0
        return pltpu.make_async_remote_copy(
            src_ref=self.out.at[t],
            dst_ref=self.arrived[side].at[t],
            send_sem=self.send.at[t],
            recv_sem=self.recv.at[side, t],
            device_id=(self.ctx, target),
            device_id_type=MESH,
        )

    def add(self, t, up):
        self.copy(t, up).wait_recv()
        self.total[...] += self.arrived[1 if up else 0][t].astype(F32)

    def step(self, s):
        me, n = self.me, self.n

        @pl.when(s >= me)
        def _():
            t = n - 1 - s + me
            self.partial(t, self.total)

            @pl.when(me > 0)
            def _():
                self.add(t, True)

            self.out[t] = self.total[...].astype(BF16)
            self.copy(t, True).start()

        @pl.when(s >= n - 1 - me)
        def _():
            t = s - (n - 1 - me)
            self.partial(t, self.total)

            @pl.when(me < n - 1)
            def _():
                self.add(t, False)

            self.out[t] = self.total[...].astype(BF16)
            self.copy(t, False).start()

    def finish(self):
        me, n = self.me, self.n
        self.partial(me, self.total)

        @pl.when(me > 0)
        def _():
            self.add(me, True)

        @pl.when(me < n - 1)
        def _():
            self.add(me, False)

        for t in range(n):

            @pl.when(t != me)
            def _():
                self.copy(t, True).wait_send()


def project_kernel(n, x_ref, gain_ref, w_ref, normed_ref, proj_ref, held, send, recv):
    ctx, me = lax.axis_index("ctx"), lax.axis_index("tp")
    rows = x_ref.shape[0]
    line_barrier(ctx, me, n, [])
    gather = LineGather(ctx, me, n, x_ref, held, send, recv)
    gather.start()

    def compute(source, origin):
        at = pl.ds(pl.multiple_of(origin * rows, rows), rows)
        piece = source[...].astype(F32)
        normed_ref[at, :] = (piece * row_scale(piece) * gain_ref[...]).astype(BF16)

        @pl.loop(0, w_ref.shape[1] // 512)
        def _(tile):
            columns = pl.ds(pl.multiple_of(tile * 512, 512), 512)
            proj_ref[at, columns] = dot(normed_ref[at, :], w_ref[:, columns]).astype(BF16)

    compute(x_ref, me)

    @pl.loop(1, n)
    def _(d):
        gather.step(d)

        @pl.when(me - d >= 0)
        def _():
            compute(held.at[me - d], me - d)

        @pl.when(me + d < n)
        def _():
            compute(held.at[me + d], me + d)

    gather.finish()


class StateSum:
    def __init__(self, ctx, me, chips, later, local, mine, pair, chip_sum, arrived, sems):
        self.chip, self.core = ctx // 2, lax.rem(ctx, 2)
        self.sibling = ctx + 1 - 2 * self.core
        self.me, self.chips, self.later = me, chips, later
        self.local, self.mine, self.pair = local, mine, pair
        self.chip_sum, self.arrived, self.sems = chip_sum, arrived, sems

    def pair_copy(self):
        return pltpu.make_async_remote_copy(
            src_ref=self.mine,
            dst_ref=self.pair,
            send_sem=self.sems.at[0, 0],
            recv_sem=self.sems.at[1, 0],
            device_id=(self.sibling, self.me),
            device_id_type=MESH,
        )

    def chip_copy(self, target, origin):
        return pltpu.make_async_remote_copy(
            src_ref=self.chip_sum,
            dst_ref=self.arrived.at[origin],
            send_sem=self.sems.at[0, target + 1],
            recv_sem=self.sems.at[1, origin + 1],
            device_id=(2 * target + self.core, self.me),
            device_id_type=MESH,
        )

    def wanted(self, source, target):
        return source > target if self.later else source < target

    def start(self):
        self.mine[...] = self.local[...].astype(BF16)
        self.pair_copy().start()

    def spread(self):
        self.pair_copy().wait()
        self.chip_sum[...] = (self.local[...] + self.pair[...].astype(F32)).astype(BF16)
        for other in range(self.chips):

            @pl.when(self.wanted(self.chip, other))
            def _():
                self.chip_copy(other, self.chip).start()

    def collect(self):
        near = self.core == (0 if self.later else 1)
        self.local[...] = jnp.where(near, self.pair[...].astype(F32), 0.0)
        for other in range(self.chips):

            @pl.when(self.wanted(other, self.chip))
            def _():
                self.chip_copy(other, other).wait_recv()
                self.local[...] += self.arrived[other].astype(F32)

            @pl.when(self.wanted(self.chip, other))
            def _():
                self.chip_copy(other, self.chip).wait_send()


def attend_kernel(
    n, chips, ctx_size,
    proj_ref, x_ref, cot_ref, wo_ref, gain_ref,
    outputs_ref, gproj_ref, mixed_ref, cots_ref,
    held, gsend, grecv,
    total, out, up_in, down_in, ssend, srecv,
    scores, attended, gatt, gkey,
    local_f, mine_f, pair_f, sum_f, arrived_f, sems_f,
    local_b, mine_b, pair_b, sum_b, arrived_b, sems_b,
):
    ctx, me = lax.axis_index("ctx"), lax.axis_index("tp")
    rows = x_ref.shape[0]
    block, width = mixed_ref.shape
    heads = width // DH
    chip, core = ctx // 2, lax.rem(ctx, 2)
    others = [ctx + 1 - 2 * core]
    others += [2 * lax.rem(chip + j, chips) + core for j in range(1, chips)]
    line_barrier(ctx, me, n, others)
    gather = LineGather(ctx, me, n, cot_ref, held, gsend, grecv)
    gather.start()
    forward = StateSum(ctx, me, chips, False, local_f, mine_f, pair_f, sum_f, arrived_f, sems_f)
    backward = StateSum(ctx, me, chips, True, local_b, mine_b, pair_b, sum_b, arrived_b, sems_b)

    def cols(h, part=0):
        return pl.ds(pl.multiple_of(part * width + h * DH, DH), DH)

    def head_rows(h):
        return pl.ds(pl.multiple_of(h * DH, DH), DH)

    def causal(value):
        down = lax.broadcasted_iota(jnp.int32, (block, block), 0)
        across = lax.broadcasted_iota(jnp.int32, (block, block), 1)
        return jnp.where(down >= across, value, 0.0).astype(BF16)

    @pl.loop(0, heads)
    def _(h):
        local_f[head_rows(h), :] = dot(proj_ref[:, cols(h, 1)], proj_ref[:, cols(h, 2)], TN)

    forward.start()

    @pl.loop(0, heads)
    def _(h):
        scores[h] = causal(dot(proj_ref[:, cols(h)], proj_ref[:, cols(h, 1)], NT))

    forward.spread()

    @pl.loop(0, heads)
    def _(h):
        attended[:, cols(h)] = dot(scores[h], proj_ref[:, cols(h, 2)])

    gather.step(1)
    forward.collect()

    @pl.loop(0, heads)
    def _(h):
        high, low = split(local_f[head_rows(h), :])
        query = proj_ref[:, cols(h)]
        value = attended[:, cols(h)] + dot(query, high) + dot(query, low)
        attended[:, cols(h)] = value
        mixed_ref[:, cols(h)] = (value * row_scale(value) * gain_ref[:, cols(h)]).astype(BF16)

    def partial(t, into):
        at = pl.ds(pl.multiple_of(t * rows, rows), rows)

        @pl.loop(0, wo_ref.shape[1] // 512)
        def _(tile):
            columns = pl.ds(pl.multiple_of(tile * 512, 512), 512)
            into[:, columns] = dot(mixed_ref[at, :], wo_ref[:, columns])

    scatter = LineScatter(ctx, me, n, partial, total, out, up_in, down_in, ssend, srecv)
    scatter.step(0)
    for d in range(2, n):
        gather.step(d)
        if d < n - 1:
            scatter.step(d - 1)

    def grad_rows(origin, source):
        at = pl.ds(pl.multiple_of(origin * rows, rows), rows)
        cots_ref[at, :] = source[...]
        weighted = dot(source[...], wo_ref[...], NT) * gain_ref[...]
        for h in range(heads):
            here = slice(h * DH, (h + 1) * DH)
            value = attended[at, here]
            scale = row_scale(value)
            part = weighted[:, here]
            mean = jnp.mean(part * value, axis=-1, keepdims=True)
            gatt[at, here] = (scale * part - scale * scale * scale * value * mean).astype(BF16)

    grad_rows(me, cot_ref)

    @pl.loop(1, n)
    def _(j):
        origin = lax.rem(me + j, n)
        grad_rows(origin, held.at[origin])

    @pl.loop(0, heads)
    def _(h):
        local_b[head_rows(h), :] = dot(proj_ref[:, cols(h)], gatt[:, cols(h)], TN)

    backward.start()
    for s in range(max(1, n - 2), n - 1):
        scatter.step(s)
    backward.spread()

    @pl.loop(0, heads)
    def _(h):
        query, key = proj_ref[:, cols(h)], proj_ref[:, cols(h, 1)]
        grad = gatt[:, cols(h)]
        gscores = causal(dot(grad, proj_ref[:, cols(h, 2)], NT))
        high, low = split(local_f[head_rows(h), :])
        gquery = dot(gscores, key) + dot(grad, high, NT) + dot(grad, low, NT)
        gproj_ref[:, cols(h)] = gquery.astype(BF16)
        gkey[:, cols(h)] = dot(gscores, query, TN)
        attended[:, cols(h)] = dot(scores[h], grad, TN)

    backward.collect()

    @pl.loop(0, heads)
    def _(h):
        high, low = split(local_b[head_rows(h), :])
        key, value = proj_ref[:, cols(h, 1)], proj_ref[:, cols(h, 2)]
        gk = gkey[:, cols(h)] + dot(value, high, NT) + dot(value, low, NT)
        gv = attended[:, cols(h)] + dot(key, high) + dot(key, low)
        gproj_ref[:, cols(h, 1)] = gk.astype(BF16)
        gproj_ref[:, cols(h, 2)] = gv.astype(BF16)

    scatter.finish()
    outputs_ref[...] = (x_ref[...].astype(F32) + total[...]).astype(BF16)
    gather.finish()


def reduce_kernel(
    n, chips, factor,
    normed_ref, gproj_ref, mixed_ref, cots_ref, w_ref, x_ref, cot_ref, gain_ref,
    igrad_ref, qgrad_ref, ograd_ref,
    total, out, up_in, down_in, ssend, srecv,
    kept, pair_out, pair_in, chip_out, chip_in, psend, precv, csend, crecv,
):
    ctx, me = lax.axis_index("ctx"), lax.axis_index("tp")
    rows = x_ref.shape[0]
    slab = qgrad_ref.shape[0]
    qwidth, owidth = gproj_ref.shape[1], mixed_ref.shape[1]
    chip, core = ctx // 2, lax.rem(ctx, 2)
    sibling = ctx + 1 - 2 * core
    others = [sibling]
    others += [2 * lax.rem(chip + j, chips) + core for j in range(1, chips)]
    line_barrier(ctx, me, n, others)

    def partial(t, into):
        at = pl.ds(pl.multiple_of(t * rows, rows), rows)

        @pl.loop(0, w_ref.shape[0] // 512)
        def _(tile):
            columns = pl.ds(pl.multiple_of(tile * 512, 512), 512)
            into[:, columns] = dot(gproj_ref[at, :], w_ref[columns, :], NT)

    def product(owner, store):
        step = max(slab, DH)
        first = pl.multiple_of((owner * slab) // step * step, step)
        shift = owner * slab - (owner * slab) // step * step

        def pieces(left, right, count, base):
            @pl.loop(0, count)
            def _(tile):
                columns = pl.ds(pl.multiple_of(tile * 512, 512), 512)
                value = dot(left[:, pl.ds(first, step)], right[:, columns], TN) * factor
                if step != slab:
                    half = value[:slab]
                    for k in range(1, step // slab):
                        half = jnp.where(shift == k * slab, value[k * slab : (k + 1) * slab], half)
                    value = half
                store(pl.ds(pl.multiple_of(base + tile * 512, 512), 512), value)

        pieces(normed_ref, gproj_ref, qwidth // 512, 0)
        pieces(cots_ref, mixed_ref, owidth // 512, qwidth)

    def pair_copy(p):
        return pltpu.make_async_remote_copy(
            src_ref=pair_out.at[p], dst_ref=pair_in.at[p],
            send_sem=psend.at[p], recv_sem=precv.at[p],
            device_id=(sibling, me), device_id_type=MESH,
        )

    def chip_copy(target, origin):
        return pltpu.make_async_remote_copy(
            src_ref=chip_out.at[target], dst_ref=chip_in.at[origin],
            send_sem=csend.at[target], recv_sem=crecv.at[origin],
            device_id=(2 * target + core, me), device_id_type=MESH,
        )

    scatter = LineScatter(ctx, me, n, partial, total, out, up_in, down_in, ssend, srecv)
    scatter.step(0)

    @pl.loop(1, chips + 1)
    def _(j):
        p = lax.rem(chip + j, chips)

        def store(columns, value):
            pair_out[p, :, columns] = value.astype(BF16)

        product(2 * p + 1 - core, store)
        pair_copy(p).start()

    @pl.loop(1, chips)
    def _(j):
        p = lax.rem(chip + j, chips)
        pair_copy(p).wait_recv()

        def store(columns, value):
            chip_out[p, :, columns] = (value + pair_in[p, :, columns].astype(F32)).astype(BF16)

        product(2 * p + core, store)
        chip_copy(p, chip).start()

    @pl.loop(1, n - 1)
    def _(s):
        scatter.step(s)

    pair_copy(chip).wait_recv()

    def keep(columns, value):
        kept[:, columns] = value + pair_in[chip, :, columns].astype(F32)

    product(2 * chip + core, keep)
    scatter.finish()
    piece = x_ref[...].astype(F32)
    scale = row_scale(piece)
    weighted = total[...] * gain_ref[...]
    mean = jnp.mean(weighted * piece, axis=-1, keepdims=True)
    igrad_ref[...] = (
        cot_ref[...].astype(F32) + scale * weighted - scale * scale * scale * piece * mean
    ).astype(BF16)

    @pl.loop(1, chips)
    def _(j):
        p = lax.rem(chip + chips - j, chips)
        chip_copy(p, p).wait_recv()
        kept[...] += chip_in[p].astype(F32)

    qgrad_ref[...] = kept[:, :qwidth]
    ograd_ref[...] = kept[:, qwidth:]

    @pl.loop(0, chips)
    def _(p):
        pair_copy(p).wait_send()

    @pl.loop(1, chips)
    def _(j):
        p = lax.rem(chip + j, chips)
        chip_copy(p, chip).wait_send()


def vmem(*shape, dtype=BF16):
    return pltpu.VMEM(shape, dtype)


def call(body, name, outs, scratch, collective, flops, operands):
    spec = pl.BlockSpec(memory_space=pltpu.VMEM)
    moved = sum(a.size * a.dtype.itemsize for a in list(operands) + list(outs))
    return pl.pallas_call(
        body,
        name=name,
        out_shape=outs,
        in_specs=[spec] * len(operands),
        out_specs=[spec] * len(outs),
        scratch_shapes=scratch,
        compiler_params=pltpu.CompilerParams(
            collective_id=collective, has_side_effects=True, vmem_limit_bytes=VMEM_LIMIT
        ),
        cost_estimate=pl.CostEstimate(flops=flops, bytes_accessed=moved, transcendentals=0),
    )(*operands)


def shards(inputs, norm_gain, qkv_weight, head_gain, out_weight, out_cotangent):
    rows, width = inputs.shape
    local_width = qkv_weight.shape[2]
    heads = local_width // DH
    n = lax.axis_size("tp")
    ctx_size = lax.axis_size("ctx")
    chips = ctx_size // 2
    block = rows * n
    slab = width // ctx_size
    factor = 1.0 / math.sqrt(block * ctx_size)
    flat_weight = qkv_weight.reshape(width, 3 * local_width)
    gain_row = norm_gain.reshape(1, width)
    head_row = head_gain.reshape(1, local_width)
    dma = pltpu.SemaphoreType.DMA
    shape = jax.ShapeDtypeStruct

    normed, projected = call(
        functools.partial(project_kernel, n),
        "project",
        [shape((block, width), BF16), shape((block, 3 * local_width), BF16)],
        [vmem(n, rows, width), dma((2, n)), dma((n,))],
        0,
        2 * block * width * 3 * local_width,
        (inputs, gain_row, flat_weight),
    )
    line_scratch = [
        vmem(rows, width, dtype=F32),
        vmem(n, rows, width),
        vmem(n, rows, width),
        vmem(n, rows, width),
        dma((n,)),
        dma((2, n)),
    ]
    state_scratch = [
        vmem(heads * DH, DH, dtype=F32),
        vmem(heads * DH, DH),
        vmem(heads * DH, DH),
        vmem(heads * DH, DH),
        vmem(chips, heads * DH, DH),
        dma((2, chips + 1)),
    ]
    outputs, grad_proj, mixed, cotangents = call(
        functools.partial(attend_kernel, n, chips, ctx_size),
        "attend",
        [
            shape((rows, width), BF16),
            shape((block, 3 * local_width), BF16),
            shape((block, local_width), BF16),
            shape((block, width), BF16),
        ],
        [vmem(n, rows, width), dma((2, n)), dma((n,))]
        + line_scratch
        + [
            vmem(heads, block, block),
            vmem(block, local_width, dtype=F32),
            vmem(block, local_width),
            vmem(block, local_width, dtype=F32),
        ]
        + state_scratch
        + state_scratch,
        1,
        4 * block * width * local_width + 14 * block * block * local_width,
        (projected, inputs, out_cotangent, out_weight, head_row),
    )
    both = 4 * local_width
    input_grad, qkv_grad, out_grad_t = call(
        functools.partial(reduce_kernel, n, chips, factor),
        "reduce",
        [
            shape((rows, width), BF16),
            shape((slab, 3 * local_width), F32),
            shape((slab, local_width), F32),
        ],
        line_scratch
        + [
            vmem(slab, both, dtype=F32),
            vmem(chips, slab, both),
            vmem(chips, slab, both),
            vmem(chips, slab, both),
            vmem(chips, slab, both),
            dma((chips,)),
            dma((chips,)),
            dma((chips,)),
            dma((chips,)),
        ],
        2,
        14 * block * width * local_width,
        (normed, grad_proj, mixed, cotangents, flat_weight, inputs, out_cotangent, gain_row),
    )
    return (outputs, input_grad, qkv_grad.reshape(slab, 3, local_width), out_grad_t)


def solution(mesh):
    in_specs = (
        P(("ctx", "tp"), None),
        P(),
        P(None, None, "tp"),
        P("tp"),
        P("tp", None),
        P(("ctx", "tp"), None),
    )
    out_specs = (
        P(("ctx", "tp"), None),
        P(("ctx", "tp"), None),
        P("ctx", None, "tp"),
        P("ctx", "tp"),
    )
    return jax.shard_map(shards, mesh=mesh, in_specs=in_specs, out_specs=out_specs, check_vma=False)
```

```python
import functools
import math

import jax
import jax.numpy as jnp
from jax import lax
from jax.experimental import pallas as pl
from jax.experimental.pallas import tpu as pltpu
from jax.sharding import PartitionSpec as P

DH = 128
EPSILON = 1e-05
MESH = pl.DeviceIdType.MESH
F32 = jnp.float32
BF16 = jnp.bfloat16
VMEM_LIMIT = 63 * 1024 * 1024
NN = (((1,), (0,)), ((), ()))
NT = (((1,), (1,)), ((), ()))
TN = (((0,), (0,)), ((), ()))


def dot(a, b, dims=NN):
    return lax.dot_general(a, b, dims, preferred_element_type=F32)


def row_scale(rows):
    return lax.rsqrt(jnp.mean(rows * rows, axis=-1, keepdims=True) + EPSILON)


def split(value):
    high = value.astype(BF16)
    return high, (value - high.astype(F32)).astype(BF16)


def line_barrier(ctx, me, n, others):
    barrier = pltpu.get_barrier_semaphore()

    @pl.when(me > 0)
    def _():
        pl.semaphore_signal(barrier, inc=1, device_id=(ctx, me - 1), device_id_type=MESH)

    @pl.when(me < n - 1)
    def _():
        pl.semaphore_signal(barrier, inc=1, device_id=(ctx, me + 1), device_id_type=MESH)

    for other in others:
        pl.semaphore_signal(barrier, inc=1, device_id=(other, me), device_id_type=MESH)
    inner = jnp.logical_and(me > 0, me < n - 1)

    @pl.when(inner)
    def _():
        pl.semaphore_wait(barrier, 2 + len(others))

    @pl.when(jnp.logical_not(inner))
    def _():
        pl.semaphore_wait(barrier, 1 + len(others))


class LineGather:
    def __init__(self, ctx, me, n, own, held, send, recv):
        self.ctx, self.me, self.n = ctx, me, n
        self.own, self.held, self.send, self.recv = own, held, send, recv

    def at(self, origin):
        rows = self.own.shape[0]
        return self.held.at[pl.ds(pl.multiple_of(origin * rows, rows), rows), :]

    def copy(self, source, origin, up):
        target = self.me + 1 if up else self.me - 1
        return pltpu.make_async_remote_copy(
            src_ref=source,
            dst_ref=self.at(origin),
            send_sem=self.send.at[1 if up else 0, origin],
            recv_sem=self.recv.at[origin],
            device_id=(self.ctx, target),
            device_id_type=MESH,
        )

    def start_up(self):
        @pl.when(self.me < self.n - 1)
        def _():
            self.copy(self.own, self.me, True).start()

    def start_down(self):
        @pl.when(self.me > 0)
        def _():
            self.copy(self.own, self.me, False).start()

    def step(self, d):
        below, above = self.me - d, self.me + d

        @pl.when(below >= 0)
        def _():
            self.copy(self.at(below), below, True).wait_recv()

            @pl.when(self.me < self.n - 1)
            def _():
                self.copy(self.at(below), below, True).start()

        @pl.when(above < self.n)
        def _():
            self.copy(self.at(above), above, False).wait_recv()

            @pl.when(self.me > 0)
            def _():
                self.copy(self.at(above), above, False).start()

    def finish(self):
        for origin in range(self.n):

            @pl.when(jnp.logical_and(origin <= self.me, self.me < self.n - 1))
            def _():
                self.copy(self.at(origin), origin, True).wait_send()

            @pl.when(jnp.logical_and(origin >= self.me, self.me > 0))
            def _():
                self.copy(self.at(origin), origin, False).wait_send()


class LineScatter:
    def __init__(self, ctx, me, n, partial, total, out, up_in, down_in, send, recv):
        self.ctx, self.me, self.n = ctx, me, n
        self.partial, self.total, self.out = partial, total, out
        self.arrived = (down_in, up_in)
        self.send, self.recv = send, recv

    def copy(self, t, up):
        target = self.me + 1 if up else self.me - 1
        side = 1 if up else 0
        return pltpu.make_async_remote_copy(
            src_ref=self.out.at[t],
            dst_ref=self.arrived[side].at[t],
            send_sem=self.send.at[t],
            recv_sem=self.recv.at[side, t],
            device_id=(self.ctx, target),
            device_id_type=MESH,
        )

    def add(self, t, up):
        self.copy(t, up).wait_recv()
        self.total[...] += self.arrived[1 if up else 0][t].astype(F32)

    def step(self, s):
        me, n = self.me, self.n

        @pl.when(s >= me)
        def _():
            t = n - 1 - s + me
            self.partial(t, self.total)

            @pl.when(me > 0)
            def _():
                self.add(t, True)

            self.out[t] = self.total[...].astype(BF16)
            self.copy(t, True).start()

        @pl.when(s >= n - 1 - me)
        def _():
            t = s - (n - 1 - me)
            self.partial(t, self.total)

            @pl.when(me < n - 1)
            def _():
                self.add(t, False)

            self.out[t] = self.total[...].astype(BF16)
            self.copy(t, False).start()

    def finish(self):
        me, n = self.me, self.n
        self.partial(me, self.total)

        @pl.when(me > 0)
        def _():
            self.add(me, True)

        @pl.when(me < n - 1)
        def _():
            self.add(me, False)

        for t in range(n):

            @pl.when(t != me)
            def _():
                self.copy(t, True).wait_send()


class StateSum:
    def __init__(self, ctx, me, chips, later, local, mine, pair, chip_sum, arrived, sems):
        self.chip, self.core = ctx // 2, lax.rem(ctx, 2)
        self.sibling = ctx + 1 - 2 * self.core
        self.me, self.chips, self.later = me, chips, later
        self.local, self.mine, self.pair = local, mine, pair
        self.chip_sum, self.arrived, self.sems = chip_sum, arrived, sems

    def pair_copy(self):
        return pltpu.make_async_remote_copy(
            src_ref=self.mine,
            dst_ref=self.pair,
            send_sem=self.sems.at[0, 0],
            recv_sem=self.sems.at[1, 0],
            device_id=(self.sibling, self.me),
            device_id_type=MESH,
        )

    def chip_copy(self, target, origin):
        return pltpu.make_async_remote_copy(
            src_ref=self.chip_sum,
            dst_ref=self.arrived.at[origin],
            send_sem=self.sems.at[0, target + 1],
            recv_sem=self.sems.at[1, origin + 1],
            device_id=(2 * target + self.core, self.me),
            device_id_type=MESH,
        )

    def wanted(self, source, target):
        return source > target if self.later else source < target

    def start(self):
        self.mine[...] = self.local[...].astype(BF16)
        self.pair_copy().start()

    def spread(self):
        self.pair_copy().wait()
        self.chip_sum[...] = (self.local[...] + self.pair[...].astype(F32)).astype(BF16)
        for other in range(self.chips):

            @pl.when(self.wanted(self.chip, other))
            def _():
                self.chip_copy(other, self.chip).start()

    def collect(self):
        near = self.core == (0 if self.later else 1)
        self.local[...] = jnp.where(near, self.pair[...].astype(F32), 0.0)
        for other in range(self.chips):

            @pl.when(self.wanted(other, self.chip))
            def _():
                self.chip_copy(other, other).wait_recv()
                self.local[...] += self.arrived[other].astype(F32)

            @pl.when(self.wanted(self.chip, other))
            def _():
                self.chip_copy(other, self.chip).wait_send()


class SlabReduce:
    def __init__(self, ctx, me, chips, factor, left, right, kept, bufs, sems):
        self.chip, self.core = ctx // 2, lax.rem(ctx, 2)
        self.sibling = ctx + 1 - 2 * self.core
        self.me, self.chips, self.factor = me, chips, factor
        self.left, self.right, self.kept = left, right, kept
        self.pair_out, self.pair_in, self.chip_out, self.chip_in = bufs
        self.sems = sems

    def product(self, owner, store):
        slab = self.kept.shape[0]
        step = max(slab, DH)
        first = pl.multiple_of((owner * slab) // step * step, step)
        shift = owner * slab - (owner * slab) // step * step

        @pl.loop(0, self.right.shape[1] // 512)
        def _(tile):
            columns = pl.ds(pl.multiple_of(tile * 512, 512), 512)
            value = dot(self.left[:, pl.ds(first, step)], self.right[:, columns], TN)
            value = value * self.factor
            if step != slab:
                part = value[:slab]
                for k in range(1, step // slab):
                    part = jnp.where(shift == k * slab, value[k * slab : (k + 1) * slab], part)
                value = part
            store(columns, value)

    def pair_copy(self, p):
        return pltpu.make_async_remote_copy(
            src_ref=self.pair_out.at[p], dst_ref=self.pair_in.at[p],
            send_sem=self.sems.at[0, p], recv_sem=self.sems.at[1, p],
            device_id=(self.sibling, self.me), device_id_type=MESH,
        )

    def chip_copy(self, target, origin):
        return pltpu.make_async_remote_copy(
            src_ref=self.chip_out.at[target], dst_ref=self.chip_in.at[origin],
            send_sem=self.sems.at[2, target], recv_sem=self.sems.at[3, origin],
            device_id=(2 * target + self.core, self.me), device_id_type=MESH,
        )

    def run(self, between=None):
        chips, chip, core = self.chips, self.chip, self.core

        @pl.loop(1, chips + 1)
        def _(j):
            p = lax.rem(chip + j, chips)

            def store(columns, value):
                self.pair_out[p, :, columns] = value.astype(BF16)

            self.product(2 * p + 1 - core, store)
            self.pair_copy(p).start()

            @pl.when(j > 1)
            def _():
                q = lax.rem(chip + j - 1, chips)
                self.pair_copy(q).wait_recv()

                def store(columns, value):
                    value = value + self.pair_in[q, :, columns].astype(F32)
                    self.chip_out[q, :, columns] = value.astype(BF16)

                self.product(2 * q + core, store)
                self.chip_copy(q, chip).start()

            if between is not None:
                between(j)

        self.pair_copy(chip).wait_recv()

        def keep(columns, value):
            self.kept[:, columns] = value + self.pair_in[chip, :, columns].astype(F32)

        self.product(2 * chip + core, keep)

    def collect(self):
        chips, chip = self.chips, self.chip

        @pl.loop(1, chips)
        def _(j):
            p = lax.rem(chip + chips - j, chips)
            self.chip_copy(p, p).wait_recv()
            self.kept[...] += self.chip_in[p].astype(F32)

    def finish(self):
        chips, chip = self.chips, self.chip

        @pl.loop(0, chips)
        def _(p):
            self.pair_copy(p).wait_send()

        @pl.loop(1, chips)
        def _(j):
            p = lax.rem(chip + j, chips)
            self.chip_copy(p, chip).wait_send()


def block_kernel(
    n, chips, factor,
    x_ref, cot_ref, in_gain_ref, gain_ref, w_hbm, wo_hbm,
    outputs_ref, igrad_ref, qgrad_ref, ograd_ref,
    w_ref, wo_ref, load,
    normed_ref, proj_ref, mixed_ref, gproj_ref,
    held_x, xsend, xrecv,
    held_c, csend, crecv,
    total,
    out_a, up_a, down_a, asend, arecv,
    out_g, up_g, down_g, gsend, grecv,
    scores, attended, gatt, gkey,
    local_f, mine_f, pair_f, sum_f, arrived_f, sems_f,
    local_b, mine_b, pair_b, sum_b, arrived_b, sems_b,
    kept_q, q0, q1, q2, q3, qsems,
    kept_o, o0, o1, o2, o3, osems,
):
    ctx, me = lax.axis_index("ctx"), lax.axis_index("tp")
    rows = x_ref.shape[0]
    block, width = mixed_ref.shape
    heads = width // DH
    chip, core = ctx // 2, lax.rem(ctx, 2)
    w_load = pltpu.make_async_copy(w_hbm, w_ref, load.at[0])
    wo_load = pltpu.make_async_copy(wo_hbm, wo_ref, load.at[1])
    w_load.start()
    wo_load.start()
    others = [ctx + 1 - 2 * core]
    others += [2 * lax.rem(chip + j, chips) + core for j in range(1, chips)]
    line_barrier(ctx, me, n, others)
    gather_x = LineGather(ctx, me, n, x_ref, held_x, xsend, xrecv)
    gather_c = LineGather(ctx, me, n, cot_ref, held_c, csend, crecv)
    forward = StateSum(ctx, me, chips, False, local_f, mine_f, pair_f, sum_f, arrived_f, sems_f)
    backward = StateSum(ctx, me, chips, True, local_b, mine_b, pair_b, sum_b, arrived_b, sems_b)
    reduce_o = SlabReduce(
        ctx, me, chips, factor, held_c, mixed_ref, kept_o, (o0, o1, o2, o3), osems
    )
    reduce_q = SlabReduce(
        ctx, me, chips, factor, normed_ref, gproj_ref, kept_q, (q0, q1, q2, q3), qsems
    )

    def row_at(origin):
        return pl.ds(pl.multiple_of(origin * rows, rows), rows)

    def cols(h, part=0):
        return pl.ds(pl.multiple_of(part * width + h * DH, DH), DH)

    def head_rows(h):
        return pl.ds(pl.multiple_of(h * DH, DH), DH)

    def causal(value):
        down = lax.broadcasted_iota(jnp.int32, (block, block), 0)
        across = lax.broadcasted_iota(jnp.int32, (block, block), 1)
        return jnp.where(down >= across, value, 0.0).astype(BF16)

    def cotangent_turn(d):
        @pl.when(me == d)
        def _():
            gather_c.start_up()

        @pl.when(me == n - 1 - d)
        def _():
            gather_c.start_down()

    def project(source, origin):
        at = row_at(origin)
        piece = source[...].astype(F32)
        normed_ref[at, :] = (piece * row_scale(piece) * in_gain_ref[...]).astype(BF16)
        for part in range(3):
            here = slice(part * width, (part + 1) * width)
            proj_ref[at, here] = dot(normed_ref[at, :], w_ref[part]).astype(BF16)

    gather_x.start_up()
    gather_x.start_down()
    cotangent_turn(0)
    held_c[row_at(me), :] = cot_ref[...]
    w_load.wait()
    project(x_ref, me)

    @pl.loop(1, n)
    def _(d):
        gather_x.step(d)
        cotangent_turn(d)

        @pl.when(me - d >= 0)
        def _():
            project(gather_x.at(me - d), me - d)

        @pl.when(me + d < n)
        def _():
            project(gather_x.at(me + d), me + d)

    @pl.loop(0, heads)
    def _(h):
        local_f[head_rows(h), :] = dot(proj_ref[:, cols(h, 1)], proj_ref[:, cols(h, 2)], TN)

    forward.start()

    @pl.loop(0, heads)
    def _(h):
        scores[h] = causal(dot(proj_ref[:, cols(h)], proj_ref[:, cols(h, 1)], NT))

    forward.spread()
    gather_c.step(1)

    @pl.loop(0, heads)
    def _(h):
        attended[:, cols(h)] = dot(scores[h], proj_ref[:, cols(h, 2)])

    forward.collect()

    @pl.loop(0, heads)
    def _(h):
        high, low = split(local_f[head_rows(h), :])
        query = proj_ref[:, cols(h)]
        value = attended[:, cols(h)] + dot(query, high) + dot(query, low)
        attended[:, cols(h)] = value
        mixed_ref[:, cols(h)] = (value * row_scale(value) * gain_ref[:, cols(h)]).astype(BF16)

    wo_load.wait()

    def out_partial(t, into):
        @pl.loop(0, wo_ref.shape[1] // 512)
        def _(tile):
            columns = pl.ds(pl.multiple_of(tile * 512, 512), 512)
            into[:, columns] = dot(mixed_ref[row_at(t), :], wo_ref[:, columns])

    scatter = LineScatter(ctx, me, n, out_partial, total, out_a, up_a, down_a, asend, arecv)
    scatter.step(0)

    def grad_rows(origin):
        at = row_at(origin)
        weighted = dot(held_c[at, :], wo_ref[...], NT) * gain_ref[...]
        for h in range(heads):
            here = slice(h * DH, (h + 1) * DH)
            value = attended[at, here]
            scale = row_scale(value)
            part = weighted[:, here]
            mean = jnp.mean(part * value, axis=-1, keepdims=True)
            gatt[at, here] = (scale * part - scale * scale * scale * value * mean).astype(BF16)

    def grad_pair(d):
        @pl.when(me - d >= 0)
        def _():
            grad_rows(me - d)

        @pl.when(me + d < n)
        def _():
            grad_rows(me + d)

    gather_c.step(2)
    grad_rows(me)

    @pl.loop(1, n - 1)
    def _(d):
        grad_pair(d)

    scatter.step(1)
    for d in range(3, n):
        gather_c.step(d)
        grad_pair(d)

    @pl.loop(0, heads)
    def _(h):
        local_b[head_rows(h), :] = dot(proj_ref[:, cols(h)], gatt[:, cols(h)], TN)

    backward.start()

    @pl.loop(0, heads)
    def _(h):
        query, key = proj_ref[:, cols(h)], proj_ref[:, cols(h, 1)]
        grad = gatt[:, cols(h)]
        gscores = causal(dot(grad, proj_ref[:, cols(h, 2)], NT))
        high, low = split(local_f[head_rows(h), :])
        gquery = dot(gscores, key) + dot(grad, high, NT) + dot(grad, low, NT)
        gproj_ref[:, cols(h)] = gquery.astype(BF16)
        gkey[:, cols(h)] = dot(gscores, query, TN)

        @pl.when(h == 0)
        def _():
            backward.spread()

    @pl.loop(0, heads)
    def _(h):
        attended[:, cols(h)] = dot(scores[h], gatt[:, cols(h)], TN)

    for s in range(2, n - 1):
        scatter.step(s)
    reduce_o.run()
    backward.collect()

    @pl.loop(0, heads)
    def _(h):
        high, low = split(local_b[head_rows(h), :])
        key, value = proj_ref[:, cols(h, 1)], proj_ref[:, cols(h, 2)]
        gk = gkey[:, cols(h)] + dot(value, high, NT) + dot(value, low, NT)
        gv = attended[:, cols(h)] + dot(key, high) + dot(key, low)
        gproj_ref[:, cols(h, 1)] = gk.astype(BF16)
        gproj_ref[:, cols(h, 2)] = gv.astype(BF16)

    scatter.finish()
    outputs_ref[...] = (x_ref[...].astype(F32) + total[...]).astype(BF16)

    def in_partial(t, into):
        at = row_at(t)

        @pl.loop(0, w_ref.shape[1] // 512)
        def _(tile):
            columns = pl.ds(pl.multiple_of(tile * 512, 512), 512)
            value = dot(gproj_ref[at, :width], w_ref[0, columns, :], NT)
            for part in range(1, 3):
                here = slice(part * width, (part + 1) * width)
                value += dot(gproj_ref[at, here], w_ref[part, columns, :], NT)
            into[:, columns] = value

    back = LineScatter(ctx, me, n, in_partial, total, out_g, up_g, down_g, gsend, grecv)
    back.step(0)

    def between(j):
        @pl.when(j == chips)
        def _():
            back.step(1)

    reduce_q.run(between)
    for s in range(2, n - 1):
        back.step(s)
    reduce_o.collect()
    ograd_ref[...] = kept_o[...]
    back.finish()
    piece = x_ref[...].astype(F32)
    scale = row_scale(piece)
    weighted = total[...] * in_gain_ref[...]
    mean = jnp.mean(weighted * piece, axis=-1, keepdims=True)
    igrad_ref[...] = (
        cot_ref[...].astype(F32) + scale * weighted - scale * scale * scale * piece * mean
    ).astype(BF16)
    reduce_q.collect()
    for part in range(3):
        qgrad_ref[part] = kept_q[:, part * width : (part + 1) * width]
    gather_x.finish()
    gather_c.finish()
    reduce_o.finish()
    reduce_q.finish()


def vmem(*shape, dtype=BF16):
    return pltpu.VMEM(shape, dtype)


def shards(inputs, norm_gain, qkv_weight, head_gain, out_weight, out_cotangent):
    rows, width = inputs.shape
    local_width = qkv_weight.shape[2]
    heads = local_width // DH
    n = lax.axis_size("tp")
    ctx_size = lax.axis_size("ctx")
    chips = ctx_size // 2
    block = rows * n
    slab = width // ctx_size
    factor = 1.0 / math.sqrt(block * ctx_size)
    dma = pltpu.SemaphoreType.DMA
    shape = jax.ShapeDtypeStruct
    gather = [vmem(block, width), dma((2, n)), dma((n,))]
    line = [vmem(n, rows, width)] * 3 + [dma((n,)), dma((2, n))]
    state = [
        vmem(heads * DH, DH, dtype=F32),
        vmem(heads * DH, DH),
        vmem(heads * DH, DH),
        vmem(heads * DH, DH),
        vmem(chips, heads * DH, DH),
        dma((2, chips + 1)),
    ]

    def slabs(columns):
        return [vmem(slab, columns, dtype=F32)] + [vmem(chips, slab, columns)] * 4 + [
            dma((4, chips))
        ]

    scratch = (
        [vmem(3, width, local_width), vmem(local_width, width), dma((2,))]
        + [vmem(block, width), vmem(block, 3 * local_width)]
        + [vmem(block, local_width), vmem(block, 3 * local_width)]
        + gather
        + gather
        + [vmem(rows, width, dtype=F32)]
        + line
        + line
        + [vmem(heads, block, block), vmem(block, local_width, dtype=F32)]
        + [vmem(block, local_width), vmem(block, local_width, dtype=F32)]
        + state
        + state
        + slabs(3 * local_width)
        + slabs(local_width)
    )
    held = pl.BlockSpec(memory_space=pltpu.VMEM)
    anywhere = pl.BlockSpec(memory_space=pl.ANY)
    outputs, input_grad, qkv_grad, out_grad_t = pl.pallas_call(
        functools.partial(block_kernel, n, chips, factor),
        name="block",
        out_shape=[
            shape((rows, width), BF16),
            shape((rows, width), BF16),
            shape((3, slab, local_width), F32),
            shape((slab, local_width), F32),
        ],
        in_specs=[held] * 4 + [anywhere] * 2,
        out_specs=[held] * 4,
        scratch_shapes=scratch,
        compiler_params=pltpu.CompilerParams(
            collective_id=0, has_side_effects=True, vmem_limit_bytes=VMEM_LIMIT
        ),
    )(
        inputs,
        out_cotangent,
        norm_gain.reshape(1, width),
        head_gain.reshape(1, local_width),
        qkv_weight.transpose(1, 0, 2),
        out_weight,
    )
    return (outputs, input_grad, qkv_grad.transpose(1, 0, 2), out_grad_t)


def solution(mesh):
    in_specs = (
        P(("ctx", "tp"), None),
        P(),
        P(None, None, "tp"),
        P("tp"),
        P("tp", None),
        P(("ctx", "tp"), None),
    )
    out_specs = (
        P(("ctx", "tp"), None),
        P(("ctx", "tp"), None),
        P("ctx", None, "tp"),
        P("ctx", "tp"),
    )
    return jax.shard_map(shards, mesh=mesh, in_specs=in_specs, out_specs=out_specs, check_vma=False)
```

```python
import functools
import math

import jax
import jax.numpy as jnp
from jax import lax
from jax.experimental import pallas as pl
from jax.experimental.pallas import tpu as pltpu
from jax.sharding import PartitionSpec as P

DH = 128
EPSILON = 1e-05
MESH = pl.DeviceIdType.MESH
F32 = jnp.float32
BF16 = jnp.bfloat16
VMEM_LIMIT = 63 * 1024 * 1024
NN = (((1,), (0,)), ((), ()))
NT = (((1,), (1,)), ((), ()))
TN = (((0,), (0,)), ((), ()))


def dot(a, b, dims=NN):
    return lax.dot_general(a, b, dims, preferred_element_type=F32)


def row_scale(rows):
    return lax.rsqrt(jnp.mean(rows * rows, axis=-1, keepdims=True) + EPSILON)


def split(value):
    high = value.astype(BF16)
    return high, (value - high.astype(F32)).astype(BF16)


def line_barrier(ctx, me, n, others):
    barrier = pltpu.get_barrier_semaphore()

    @pl.when(me > 0)
    def _():
        pl.semaphore_signal(barrier, inc=1, device_id=(ctx, me - 1), device_id_type=MESH)

    @pl.when(me < n - 1)
    def _():
        pl.semaphore_signal(barrier, inc=1, device_id=(ctx, me + 1), device_id_type=MESH)

    for other in others:
        pl.semaphore_signal(barrier, inc=1, device_id=(other, me), device_id_type=MESH)
    inner = jnp.logical_and(me > 0, me < n - 1)

    @pl.when(inner)
    def _():
        pl.semaphore_wait(barrier, 2 + len(others))

    @pl.when(jnp.logical_not(inner))
    def _():
        pl.semaphore_wait(barrier, 1 + len(others))


class LineGather:
    def __init__(self, ctx, me, n, own, held, send, recv):
        self.ctx, self.me, self.n = ctx, me, n
        self.own, self.held, self.send, self.recv = own, held, send, recv

    def at(self, origin):
        rows = self.own.shape[0]
        return self.held.at[pl.ds(pl.multiple_of(origin * rows, rows), rows), :]

    def copy(self, source, origin, up):
        target = self.me + 1 if up else self.me - 1
        return pltpu.make_async_remote_copy(
            src_ref=source,
            dst_ref=self.at(origin),
            send_sem=self.send.at[1 if up else 0, origin],
            recv_sem=self.recv.at[origin],
            device_id=(self.ctx, target),
            device_id_type=MESH,
        )

    def start_up(self):
        @pl.when(self.me < self.n - 1)
        def _():
            self.copy(self.own, self.me, True).start()

    def start_down(self):
        @pl.when(self.me > 0)
        def _():
            self.copy(self.own, self.me, False).start()

    def step(self, d):
        below, above = self.me - d, self.me + d

        @pl.when(below >= 0)
        def _():
            self.copy(self.at(below), below, True).wait_recv()

            @pl.when(self.me < self.n - 1)
            def _():
                self.copy(self.at(below), below, True).start()

        @pl.when(above < self.n)
        def _():
            self.copy(self.at(above), above, False).wait_recv()

            @pl.when(self.me > 0)
            def _():
                self.copy(self.at(above), above, False).start()

    def finish(self):
        for origin in range(self.n):

            @pl.when(jnp.logical_and(origin <= self.me, self.me < self.n - 1))
            def _():
                self.copy(self.at(origin), origin, True).wait_send()

            @pl.when(jnp.logical_and(origin >= self.me, self.me > 0))
            def _():
                self.copy(self.at(origin), origin, False).wait_send()


class LineScatter:
    def __init__(self, ctx, me, n, partial, total, out, up_in, down_in, send, recv):
        self.ctx, self.me, self.n = ctx, me, n
        self.partial, self.total, self.out = partial, total, out
        self.arrived = (down_in, up_in)
        self.send, self.recv = send, recv

    def copy(self, t, up):
        target = self.me + 1 if up else self.me - 1
        side = 1 if up else 0
        return pltpu.make_async_remote_copy(
            src_ref=self.out.at[t],
            dst_ref=self.arrived[side].at[t],
            send_sem=self.send.at[t],
            recv_sem=self.recv.at[side, t],
            device_id=(self.ctx, target),
            device_id_type=MESH,
        )

    def add(self, t, up):
        self.copy(t, up).wait_recv()
        self.total[...] += self.arrived[1 if up else 0][t].astype(F32)

    def step(self, s):
        me, n = self.me, self.n

        @pl.when(s >= me)
        def _():
            t = n - 1 - s + me
            self.partial(t, self.total)

            @pl.when(me > 0)
            def _():
                self.add(t, True)

            self.out[t] = self.total[...].astype(BF16)
            self.copy(t, True).start()

        @pl.when(s >= n - 1 - me)
        def _():
            t = s - (n - 1 - me)
            self.partial(t, self.total)

            @pl.when(me < n - 1)
            def _():
                self.add(t, False)

            self.out[t] = self.total[...].astype(BF16)
            self.copy(t, False).start()

    def finish(self):
        me, n = self.me, self.n
        self.partial(me, self.total)

        @pl.when(me > 0)
        def _():
            self.add(me, True)

        @pl.when(me < n - 1)
        def _():
            self.add(me, False)

        for t in range(n):

            @pl.when(t != me)
            def _():
                self.copy(t, True).wait_send()


class StateSum:
    def __init__(self, ctx, me, chips, later, local, mine, pair, chip_sum, arrived, sems):
        self.chip, self.core = ctx // 2, lax.rem(ctx, 2)
        self.sibling = ctx + 1 - 2 * self.core
        self.me, self.chips, self.later = me, chips, later
        self.local, self.mine, self.pair = local, mine, pair
        self.chip_sum, self.arrived, self.sems = chip_sum, arrived, sems

    def pair_copy(self):
        return pltpu.make_async_remote_copy(
            src_ref=self.mine,
            dst_ref=self.pair,
            send_sem=self.sems.at[0, 0],
            recv_sem=self.sems.at[1, 0],
            device_id=(self.sibling, self.me),
            device_id_type=MESH,
        )

    def chip_copy(self, target, origin):
        return pltpu.make_async_remote_copy(
            src_ref=self.chip_sum,
            dst_ref=self.arrived.at[origin],
            send_sem=self.sems.at[0, target + 1],
            recv_sem=self.sems.at[1, origin + 1],
            device_id=(2 * target + self.core, self.me),
            device_id_type=MESH,
        )

    def wanted(self, source, target):
        return source > target if self.later else source < target

    def start(self):
        self.mine[...] = self.local[...].astype(BF16)
        self.pair_copy().start()

    def spread(self):
        self.pair_copy().wait()
        self.chip_sum[...] = (self.local[...] + self.pair[...].astype(F32)).astype(BF16)
        for other in range(self.chips):

            @pl.when(self.wanted(self.chip, other))
            def _():
                self.chip_copy(other, self.chip).start()

    def collect(self):
        near = self.core == (0 if self.later else 1)
        self.local[...] = jnp.where(near, self.pair[...].astype(F32), 0.0)
        for other in range(self.chips):

            @pl.when(self.wanted(other, self.chip))
            def _():
                self.chip_copy(other, other).wait_recv()
                self.local[...] += self.arrived[other].astype(F32)

            @pl.when(self.wanted(self.chip, other))
            def _():
                self.chip_copy(other, self.chip).wait_send()


class SlabReduce:
    def __init__(self, ctx, me, chips, factor, left, right, base, kept, bufs, sems):
        self.chip, self.core = ctx // 2, lax.rem(ctx, 2)
        self.sibling = ctx + 1 - 2 * self.core
        self.me, self.chips, self.factor = me, chips, factor
        self.left, self.right, self.base, self.kept = left, right, base, kept
        self.pair_out, self.pair_in, self.chip_out, self.chip_in = bufs
        self.sems = sems

    def product(self, owner, store):
        slab = self.kept.shape[0]
        step = max(slab, DH)
        first = pl.multiple_of((owner * slab) // step * step, step)
        shift = owner * slab - (owner * slab) // step * step

        @pl.loop(0, self.kept.shape[1] // 512)
        def _(tile):
            columns = pl.ds(pl.multiple_of(tile * 512, 512), 512)
            source = pl.ds(pl.multiple_of(self.base + tile * 512, 512), 512)
            value = dot(self.left[:, pl.ds(first, step)], self.right[:, source], TN)
            value = value * self.factor
            if step != slab:
                part = value[:slab]
                for k in range(1, step // slab):
                    part = jnp.where(shift == k * slab, value[k * slab : (k + 1) * slab], part)
                value = part
            store(columns, value)

    def pair_copy(self, p):
        return pltpu.make_async_remote_copy(
            src_ref=self.pair_out.at[p], dst_ref=self.pair_in.at[p],
            send_sem=self.sems.at[0, p], recv_sem=self.sems.at[1, p],
            device_id=(self.sibling, self.me), device_id_type=MESH,
        )

    def chip_copy(self, target, origin):
        return pltpu.make_async_remote_copy(
            src_ref=self.chip_out.at[target], dst_ref=self.chip_in.at[origin],
            send_sem=self.sems.at[2, target], recv_sem=self.sems.at[3, origin],
            device_id=(2 * target + self.core, self.me), device_id_type=MESH,
        )

    def to_pair(self, p):
        def store(columns, value):
            self.pair_out[p, :, columns] = value.astype(BF16)

        self.product(2 * p + 1 - self.core, store)
        self.pair_copy(p).start()

    def to_chip(self, q):
        self.pair_copy(q).wait_recv()

        def store(columns, value):
            value = value + self.pair_in[q, :, columns].astype(F32)
            self.chip_out[q, :, columns] = value.astype(BF16)

        self.product(2 * q + self.core, store)
        self.chip_copy(q, self.chip).start()

    def keep_own(self):
        self.pair_copy(self.chip).wait_recv()

        def keep(columns, value):
            self.kept[:, columns] = value + self.pair_in[self.chip, :, columns].astype(F32)

        self.product(2 * self.chip + self.core, keep)

    def collect(self):
        chips, chip = self.chips, self.chip

        @pl.loop(1, chips)
        def _(j):
            p = lax.rem(chip + chips - j, chips)
            self.chip_copy(p, p).wait_recv()
            self.kept[...] += self.chip_in[p].astype(F32)

    def finish(self):
        chips, chip = self.chips, self.chip

        @pl.loop(0, chips)
        def _(p):
            self.pair_copy(p).wait_send()

        @pl.loop(1, chips)
        def _(j):
            p = lax.rem(chip + j, chips)
            self.chip_copy(p, chip).wait_send()


def run_slabs(parts, between=None):
    chips, chip = parts[0].chips, parts[0].chip

    @pl.loop(1, chips + 1)
    def _(j):
        for part in parts:
            part.to_pair(lax.rem(chip + j, chips))

        @pl.when(j > 1)
        def _():
            for part in parts:
                part.to_chip(lax.rem(chip + j - 1, chips))

        if between is not None:
            between(j)


def block_kernel(
    n, chips, factor,
    x_ref, cot_ref, in_gain_ref, gain_ref, w_hbm, wo_hbm,
    outputs_ref, igrad_ref, qgrad_ref, ograd_ref,
    w_ref, wo_ref, load,
    normed_ref, proj_ref, mixed_ref, gproj_ref,
    held_x, xsend, xrecv,
    held_c, csend, crecv,
    total,
    out_a, up_a, down_a, asend, arecv,
    out_g, up_g, down_g, gsend, grecv,
    scores, attended, gatt, gkey,
    local_f, mine_f, pair_f, sum_f, arrived_f, sems_f,
    local_b, mine_b, pair_b, sum_b, arrived_b, sems_b,
    kept_q, q0, q1, q2, q3, qsems,
    kept_k, k0, k1, k2, k3, ksems,
    kept_o, o0, o1, o2, o3, osems,
):
    ctx, me = lax.axis_index("ctx"), lax.axis_index("tp")
    rows = x_ref.shape[0]
    block, width = mixed_ref.shape
    heads = width // DH
    chip, core = ctx // 2, lax.rem(ctx, 2)
    w_load = pltpu.make_async_copy(w_hbm, w_ref, load.at[0])
    wo_load = pltpu.make_async_copy(wo_hbm, wo_ref, load.at[1])
    w_load.start()
    wo_load.start()
    others = [ctx + 1 - 2 * core]
    others += [2 * lax.rem(chip + j, chips) + core for j in range(1, chips)]
    line_barrier(ctx, me, n, others)
    gather_x = LineGather(ctx, me, n, x_ref, held_x, xsend, xrecv)
    gather_c = LineGather(ctx, me, n, cot_ref, held_c, csend, crecv)
    forward = StateSum(ctx, me, chips, False, local_f, mine_f, pair_f, sum_f, arrived_f, sems_f)
    backward = StateSum(ctx, me, chips, True, local_b, mine_b, pair_b, sum_b, arrived_b, sems_b)
    reduce_o = SlabReduce(
        ctx, me, chips, factor, held_c, mixed_ref, 0, kept_o, (o0, o1, o2, o3), osems
    )
    reduce_q = SlabReduce(
        ctx, me, chips, factor, normed_ref, gproj_ref, 0, kept_q, (q0, q1, q2, q3), qsems
    )
    reduce_k = SlabReduce(
        ctx, me, chips, factor, normed_ref, gproj_ref, width, kept_k, (k0, k1, k2, k3), ksems
    )

    def row_at(origin):
        return pl.ds(pl.multiple_of(origin * rows, rows), rows)

    def cols(h, part=0):
        return pl.ds(pl.multiple_of(part * width + h * DH, DH), DH)

    def head_rows(h):
        return pl.ds(pl.multiple_of(h * DH, DH), DH)

    def causal(value):
        down = lax.broadcasted_iota(jnp.int32, (block, block), 0)
        across = lax.broadcasted_iota(jnp.int32, (block, block), 1)
        return jnp.where(down >= across, value, 0.0).astype(BF16)

    def cotangent_turn(d):
        @pl.when(me == d)
        def _():
            gather_c.start_up()

        @pl.when(me == n - 1 - d)
        def _():
            gather_c.start_down()

    def project(source, origin):
        at = row_at(origin)
        piece = source[...].astype(F32)
        normed_ref[at, :] = (piece * row_scale(piece) * in_gain_ref[...]).astype(BF16)
        for part in range(3):
            here = slice(part * width, (part + 1) * width)
            proj_ref[at, here] = dot(normed_ref[at, :], w_ref[part]).astype(BF16)

    gather_x.start_up()
    gather_x.start_down()
    cotangent_turn(0)
    held_c[row_at(me), :] = cot_ref[...]
    w_load.wait()
    project(x_ref, me)

    @pl.loop(1, n)
    def _(d):
        gather_x.step(d)
        cotangent_turn(d)

        @pl.when(me - d >= 0)
        def _():
            project(gather_x.at(me - d), me - d)

        @pl.when(me + d < n)
        def _():
            project(gather_x.at(me + d), me + d)

    @pl.loop(0, heads)
    def _(h):
        local_f[head_rows(h), :] = dot(proj_ref[:, cols(h, 1)], proj_ref[:, cols(h, 2)], TN)

    forward.start()

    @pl.loop(0, heads)
    def _(h):
        scores[h] = causal(dot(proj_ref[:, cols(h)], proj_ref[:, cols(h, 1)], NT))

    forward.spread()
    gather_c.step(1)

    @pl.loop(0, heads)
    def _(h):
        attended[:, cols(h)] = dot(scores[h], proj_ref[:, cols(h, 2)])

    forward.collect()

    @pl.loop(0, heads)
    def _(h):
        high, low = split(local_f[head_rows(h), :])
        query = proj_ref[:, cols(h)]
        value = attended[:, cols(h)] + dot(query, high) + dot(query, low)
        attended[:, cols(h)] = value
        mixed_ref[:, cols(h)] = (value * row_scale(value) * gain_ref[:, cols(h)]).astype(BF16)

    wo_load.wait()

    def out_partial(t, into):
        @pl.loop(0, wo_ref.shape[1] // 512)
        def _(tile):
            columns = pl.ds(pl.multiple_of(tile * 512, 512), 512)
            into[:, columns] = dot(mixed_ref[row_at(t), :], wo_ref[:, columns])

    scatter = LineScatter(ctx, me, n, out_partial, total, out_a, up_a, down_a, asend, arecv)
    scatter.step(0)

    def grad_rows(origin):
        at = row_at(origin)
        weighted = dot(held_c[at, :], wo_ref[...], NT) * gain_ref[...]
        for h in range(heads):
            here = slice(h * DH, (h + 1) * DH)
            value = attended[at, here]
            scale = row_scale(value)
            part = weighted[:, here]
            mean = jnp.mean(part * value, axis=-1, keepdims=True)
            gatt[at, here] = (scale * part - scale * scale * scale * value * mean).astype(BF16)

    def grad_pair(d):
        @pl.when(me - d >= 0)
        def _():
            grad_rows(me - d)

        @pl.when(me + d < n)
        def _():
            grad_rows(me + d)

    gather_c.step(2)
    grad_rows(me)

    @pl.loop(1, n - 1)
    def _(d):
        grad_pair(d)

    scatter.step(1)
    for d in range(3, n):
        gather_c.step(d)
        grad_pair(d)

    @pl.loop(0, heads)
    def _(h):
        local_b[head_rows(h), :] = dot(proj_ref[:, cols(h)], gatt[:, cols(h)], TN)

    backward.start()

    @pl.loop(0, heads)
    def _(h):
        query, key = proj_ref[:, cols(h)], proj_ref[:, cols(h, 1)]
        grad = gatt[:, cols(h)]
        gscores = causal(dot(grad, proj_ref[:, cols(h, 2)], NT))
        high, low = split(local_f[head_rows(h), :])
        gquery = dot(gscores, key) + dot(grad, high, NT) + dot(grad, low, NT)
        gproj_ref[:, cols(h)] = gquery.astype(BF16)
        gkey[:, cols(h)] = dot(gscores, query, TN)

        @pl.when(h == 0)
        def _():
            backward.spread()

    @pl.loop(0, heads)
    def _(h):
        attended[:, cols(h)] = dot(scores[h], gatt[:, cols(h)], TN)

    for s in range(2, n - 1):
        scatter.step(s)
    run_slabs([reduce_o, reduce_q])
    backward.collect()

    @pl.loop(0, heads)
    def _(h):
        high, low = split(local_b[head_rows(h), :])
        key, value = proj_ref[:, cols(h, 1)], proj_ref[:, cols(h, 2)]
        gk = gkey[:, cols(h)] + dot(value, high, NT) + dot(value, low, NT)
        gv = attended[:, cols(h)] + dot(key, high) + dot(key, low)
        gproj_ref[:, cols(h, 1)] = gk.astype(BF16)
        gproj_ref[:, cols(h, 2)] = gv.astype(BF16)

    def in_partial(t, into):
        at = row_at(t)

        @pl.loop(0, w_ref.shape[1] // 512)
        def _(tile):
            columns = pl.ds(pl.multiple_of(tile * 512, 512), 512)
            value = dot(gproj_ref[at, :width], w_ref[0, columns, :], NT)
            for part in range(1, 3):
                here = slice(part * width, (part + 1) * width)
                value += dot(gproj_ref[at, here], w_ref[part, columns, :], NT)
            into[:, columns] = value

    back = LineScatter(ctx, me, n, in_partial, total, out_g, up_g, down_g, gsend, grecv)
    back.step(0)

    def between(j):
        @pl.when(j == chips)
        def _():
            back.step(1)

    run_slabs([reduce_k], between)
    reduce_k.keep_own()
    scatter.finish()
    outputs_ref[...] = (x_ref[...].astype(F32) + total[...]).astype(BF16)
    for s in range(2, n - 1):
        back.step(s)
    reduce_o.keep_own()
    reduce_q.keep_own()
    reduce_o.collect()
    ograd_ref[...] = kept_o[...]
    reduce_q.collect()
    qgrad_ref[0] = kept_q[...]
    back.finish()
    piece = x_ref[...].astype(F32)
    scale = row_scale(piece)
    weighted = total[...] * in_gain_ref[...]
    mean = jnp.mean(weighted * piece, axis=-1, keepdims=True)
    igrad_ref[...] = (
        cot_ref[...].astype(F32) + scale * weighted - scale * scale * scale * piece * mean
    ).astype(BF16)
    reduce_k.collect()
    for part in range(2):
        qgrad_ref[part + 1] = kept_k[:, part * width : (part + 1) * width]
    gather_x.finish()
    gather_c.finish()
    reduce_o.finish()
    reduce_q.finish()
    reduce_k.finish()


def vmem(*shape, dtype=BF16):
    return pltpu.VMEM(shape, dtype)


def shards(inputs, norm_gain, qkv_weight, head_gain, out_weight, out_cotangent):
    rows, width = inputs.shape
    local_width = qkv_weight.shape[2]
    heads = local_width // DH
    n = lax.axis_size("tp")
    ctx_size = lax.axis_size("ctx")
    chips = ctx_size // 2
    block = rows * n
    slab = width // ctx_size
    factor = 1.0 / math.sqrt(block * ctx_size)
    dma = pltpu.SemaphoreType.DMA
    shape = jax.ShapeDtypeStruct
    gather = [vmem(block, width), dma((2, n)), dma((n,))]
    line = [vmem(n, rows, width)] * 3 + [dma((n,)), dma((2, n))]
    state = [
        vmem(heads * DH, DH, dtype=F32),
        vmem(heads * DH, DH),
        vmem(heads * DH, DH),
        vmem(heads * DH, DH),
        vmem(chips, heads * DH, DH),
        dma((2, chips + 1)),
    ]

    def slabs(columns):
        return [vmem(slab, columns, dtype=F32)] + [vmem(chips, slab, columns)] * 4 + [
            dma((4, chips))
        ]

    scratch = (
        [vmem(3, width, local_width), vmem(local_width, width), dma((2,))]
        + [vmem(block, width), vmem(block, 3 * local_width)]
        + [vmem(block, local_width), vmem(block, 3 * local_width)]
        + gather
        + gather
        + [vmem(rows, width, dtype=F32)]
        + line
        + line
        + [vmem(heads, block, block), vmem(block, local_width, dtype=F32)]
        + [vmem(block, local_width), vmem(block, local_width, dtype=F32)]
        + state
        + state
        + slabs(local_width)
        + slabs(2 * local_width)
        + slabs(local_width)
    )
    held = pl.BlockSpec(memory_space=pltpu.VMEM)
    anywhere = pl.BlockSpec(memory_space=pl.ANY)
    outputs, input_grad, qkv_grad, out_grad_t = pl.pallas_call(
        functools.partial(block_kernel, n, chips, factor),
        name="block",
        out_shape=[
            shape((rows, width), BF16),
            shape((rows, width), BF16),
            shape((3, slab, local_width), F32),
            shape((slab, local_width), F32),
        ],
        in_specs=[held] * 4 + [anywhere] * 2,
        out_specs=[held] * 4,
        scratch_shapes=scratch,
        compiler_params=pltpu.CompilerParams(
            collective_id=0, has_side_effects=True, vmem_limit_bytes=VMEM_LIMIT
        ),
    )(
        inputs,
        out_cotangent,
        norm_gain.reshape(1, width),
        head_gain.reshape(1, local_width),
        qkv_weight.transpose(1, 0, 2),
        out_weight,
    )
    return (outputs, input_grad, qkv_grad.transpose(1, 0, 2), out_grad_t)


def solution(mesh):
    in_specs = (
        P(("ctx", "tp"), None),
        P(),
        P(None, None, "tp"),
        P("tp"),
        P("tp", None),
        P(("ctx", "tp"), None),
    )
    out_specs = (
        P(("ctx", "tp"), None),
        P(("ctx", "tp"), None),
        P("ctx", None, "tp"),
        P("ctx", "tp"),
    )
    return jax.shard_map(shards, mesh=mesh, in_specs=in_specs, out_specs=out_specs, check_vma=False)
```

```python
import functools
import math

import jax
import jax.numpy as jnp
from jax import lax
from jax.experimental import pallas as pl
from jax.experimental.pallas import tpu as pltpu
from jax.sharding import PartitionSpec as P

DH = 128
EPSILON = 1e-05
MESH = pl.DeviceIdType.MESH
F32 = jnp.float32
BF16 = jnp.bfloat16
VMEM_LIMIT = 63 * 1024 * 1024
NN = (((1,), (0,)), ((), ()))
NT = (((1,), (1,)), ((), ()))
TN = (((0,), (0,)), ((), ()))


def dot(a, b, dims=NN):
    return lax.dot_general(a, b, dims, preferred_element_type=F32)


def row_scale(rows):
    return lax.rsqrt(jnp.mean(rows * rows, axis=-1, keepdims=True) + EPSILON)


def split(value):
    high = value.astype(BF16)
    return high, (value - high.astype(F32)).astype(BF16)


def line_barrier(ctx, me, n, others):
    barrier = pltpu.get_barrier_semaphore()

    @pl.when(me > 0)
    def _():
        pl.semaphore_signal(barrier, inc=1, device_id=(ctx, me - 1), device_id_type=MESH)

    @pl.when(me < n - 1)
    def _():
        pl.semaphore_signal(barrier, inc=1, device_id=(ctx, me + 1), device_id_type=MESH)

    for other in others:
        pl.semaphore_signal(barrier, inc=1, device_id=(other, me), device_id_type=MESH)
    inner = jnp.logical_and(me > 0, me < n - 1)

    @pl.when(inner)
    def _():
        pl.semaphore_wait(barrier, 2 + len(others))

    @pl.when(jnp.logical_not(inner))
    def _():
        pl.semaphore_wait(barrier, 1 + len(others))


class LineGather:
    def __init__(self, ctx, me, n, own, held, send, recv):
        self.ctx, self.me, self.n = ctx, me, n
        self.own, self.held, self.send, self.recv = own, held, send, recv

    def at(self, origin):
        rows = self.own.shape[0]
        return self.held.at[pl.ds(pl.multiple_of(origin * rows, rows), rows), :]

    def copy(self, source, origin, up):
        target = self.me + 1 if up else self.me - 1
        return pltpu.make_async_remote_copy(
            src_ref=source,
            dst_ref=self.at(origin),
            send_sem=self.send.at[1 if up else 0, origin],
            recv_sem=self.recv.at[origin],
            device_id=(self.ctx, target),
            device_id_type=MESH,
        )

    def start_up(self):
        @pl.when(self.me < self.n - 1)
        def _():
            self.copy(self.own, self.me, True).start()

    def start_down(self):
        @pl.when(self.me > 0)
        def _():
            self.copy(self.own, self.me, False).start()

    def step(self, d):
        below, above = self.me - d, self.me + d

        @pl.when(below >= 0)
        def _():
            self.copy(self.at(below), below, True).wait_recv()

            @pl.when(self.me < self.n - 1)
            def _():
                self.copy(self.at(below), below, True).start()

        @pl.when(above < self.n)
        def _():
            self.copy(self.at(above), above, False).wait_recv()

            @pl.when(self.me > 0)
            def _():
                self.copy(self.at(above), above, False).start()

    def finish(self):
        for origin in range(self.n):

            @pl.when(jnp.logical_and(origin <= self.me, self.me < self.n - 1))
            def _():
                self.copy(self.at(origin), origin, True).wait_send()

            @pl.when(jnp.logical_and(origin >= self.me, self.me > 0))
            def _():
                self.copy(self.at(origin), origin, False).wait_send()


class LineScatter:
    def __init__(self, ctx, me, n, partial, total, out, up_in, down_in, send, recv):
        self.ctx, self.me, self.n = ctx, me, n
        self.partial, self.total, self.out = partial, total, out
        self.arrived = (down_in, up_in)
        self.send, self.recv = send, recv

    def copy(self, t, up):
        target = self.me + 1 if up else self.me - 1
        side = 1 if up else 0
        return pltpu.make_async_remote_copy(
            src_ref=self.out.at[t],
            dst_ref=self.arrived[side].at[t],
            send_sem=self.send.at[t],
            recv_sem=self.recv.at[side, t],
            device_id=(self.ctx, target),
            device_id_type=MESH,
        )

    def add(self, t, up):
        self.copy(t, up).wait_recv()
        self.total[...] += self.arrived[1 if up else 0][t].astype(F32)

    def step(self, s):
        me, n = self.me, self.n

        @pl.when(s >= me)
        def _():
            t = n - 1 - s + me
            self.partial(t, self.total)

            @pl.when(me > 0)
            def _():
                self.add(t, True)

            self.out[t] = self.total[...].astype(BF16)
            self.copy(t, True).start()

        @pl.when(s >= n - 1 - me)
        def _():
            t = s - (n - 1 - me)
            self.partial(t, self.total)

            @pl.when(me < n - 1)
            def _():
                self.add(t, False)

            self.out[t] = self.total[...].astype(BF16)
            self.copy(t, False).start()

    def finish(self):
        me, n = self.me, self.n
        self.partial(me, self.total)

        @pl.when(me > 0)
        def _():
            self.add(me, True)

        @pl.when(me < n - 1)
        def _():
            self.add(me, False)

        for t in range(n):

            @pl.when(t != me)
            def _():
                self.copy(t, True).wait_send()


class StateSum:
    def __init__(self, ctx, me, chips, later, local, mine, pair, chip_sum, arrived, sems):
        self.chip, self.core = ctx // 2, lax.rem(ctx, 2)
        self.sibling = ctx + 1 - 2 * self.core
        self.me, self.chips, self.later = me, chips, later
        self.local, self.mine, self.pair = local, mine, pair
        self.chip_sum, self.arrived, self.sems = chip_sum, arrived, sems

    def pair_copy(self):
        return pltpu.make_async_remote_copy(
            src_ref=self.mine,
            dst_ref=self.pair,
            send_sem=self.sems.at[0, 0],
            recv_sem=self.sems.at[1, 0],
            device_id=(self.sibling, self.me),
            device_id_type=MESH,
        )

    def chip_copy(self, target, origin):
        return pltpu.make_async_remote_copy(
            src_ref=self.chip_sum,
            dst_ref=self.arrived.at[origin],
            send_sem=self.sems.at[0, target + 1],
            recv_sem=self.sems.at[1, origin + 1],
            device_id=(2 * target + self.core, self.me),
            device_id_type=MESH,
        )

    def wanted(self, source, target):
        return source > target if self.later else source < target

    def start(self):
        self.mine[...] = self.local[...].astype(BF16)
        self.pair_copy().start()

    def spread(self):
        self.pair_copy().wait()
        self.chip_sum[...] = (self.local[...] + self.pair[...].astype(F32)).astype(BF16)
        for other in range(self.chips):

            @pl.when(self.wanted(self.chip, other))
            def _():
                self.chip_copy(other, self.chip).start()

    def collect(self):
        near = self.core == (0 if self.later else 1)
        self.local[...] = jnp.where(near, self.pair[...].astype(F32), 0.0)
        for other in range(self.chips):

            @pl.when(self.wanted(other, self.chip))
            def _():
                self.chip_copy(other, other).wait_recv()
                self.local[...] += self.arrived[other].astype(F32)

            @pl.when(self.wanted(self.chip, other))
            def _():
                self.chip_copy(other, self.chip).wait_send()


class SlabReduce:
    def __init__(self, ctx, me, chips, factor, left, right, base, kept, bufs, sems):
        self.chip, self.core = ctx // 2, lax.rem(ctx, 2)
        self.sibling = ctx + 1 - 2 * self.core
        self.me, self.chips, self.factor = me, chips, factor
        self.left, self.right, self.base, self.kept = left, right, base, kept
        self.pair_out, self.pair_in, self.chip_out, self.chip_in = bufs
        self.sems = sems

    def product(self, owner, store):
        slab = self.kept.shape[0]
        step = max(slab, DH)
        first = pl.multiple_of((owner * slab) // step * step, step)
        shift = owner * slab - (owner * slab) // step * step

        @pl.loop(0, self.kept.shape[1] // 512)
        def _(tile):
            columns = pl.ds(pl.multiple_of(tile * 512, 512), 512)
            source = pl.ds(pl.multiple_of(self.base + tile * 512, 512), 512)
            value = dot(self.left[:, pl.ds(first, step)], self.right[:, source], TN)
            value = value * self.factor
            if step != slab:
                part = value[:slab]
                for k in range(1, step // slab):
                    part = jnp.where(shift == k * slab, value[k * slab : (k + 1) * slab], part)
                value = part
            store(columns, value)

    def pair_copy(self, p):
        return pltpu.make_async_remote_copy(
            src_ref=self.pair_out.at[p], dst_ref=self.pair_in.at[p],
            send_sem=self.sems.at[0, p], recv_sem=self.sems.at[1, p],
            device_id=(self.sibling, self.me), device_id_type=MESH,
        )

    def chip_copy(self, target, origin):
        return pltpu.make_async_remote_copy(
            src_ref=self.chip_out.at[target], dst_ref=self.chip_in.at[origin],
            send_sem=self.sems.at[2, target], recv_sem=self.sems.at[3, origin],
            device_id=(2 * target + self.core, self.me), device_id_type=MESH,
        )

    def to_pair(self, p):
        def store(columns, value):
            self.pair_out[p, :, columns] = value.astype(BF16)

        self.product(2 * p + 1 - self.core, store)
        self.pair_copy(p).start()

    def to_chip(self, q):
        self.pair_copy(q).wait_recv()

        def store(columns, value):
            value = value + self.pair_in[q, :, columns].astype(F32)
            self.chip_out[q, :, columns] = value.astype(BF16)

        self.product(2 * q + self.core, store)
        self.chip_copy(q, self.chip).start()

    def keep_own(self):
        self.pair_copy(self.chip).wait_recv()

        def keep(columns, value):
            self.kept[:, columns] = value + self.pair_in[self.chip, :, columns].astype(F32)

        self.product(2 * self.chip + self.core, keep)

    def collect(self, first=1, last=None):
        chips, chip = self.chips, self.chip

        @pl.loop(first, chips if last is None else last)
        def _(j):
            p = lax.rem(chip + chips - j, chips)
            self.chip_copy(p, p).wait_recv()
            self.kept[...] += self.chip_in[p].astype(F32)

    def finish(self):
        chips, chip = self.chips, self.chip

        @pl.loop(0, chips)
        def _(p):
            self.pair_copy(p).wait_send()

        @pl.loop(1, chips)
        def _(j):
            p = lax.rem(chip + j, chips)
            self.chip_copy(p, chip).wait_send()


def run_slabs(parts, between=None):
    chips, chip = parts[0].chips, parts[0].chip

    @pl.loop(1, chips + 1)
    def _(j):
        for part in parts:
            part.to_pair(lax.rem(chip + j, chips))

        @pl.when(j > 1)
        def _():
            for part in parts:
                part.to_chip(lax.rem(chip + j - 1, chips))

        if between is not None:
            between(j)


def block_kernel(
    n, chips, factor,
    x_ref, cot_ref, in_gain_ref, gain_ref, w_hbm, wo_hbm,
    outputs_ref, igrad_ref, qgrad_ref, ograd_ref,
    w_ref, wo_ref, load,
    normed_ref, proj_ref, mixed_ref, gproj_ref,
    held_x, xsend, xrecv,
    held_c, csend, crecv,
    total,
    out_a, up_a, down_a, asend, arecv,
    out_g, up_g, down_g, gsend, grecv,
    scores, attended, gatt, gkey,
    local_f, mine_f, pair_f, sum_f, arrived_f, sems_f,
    local_b, mine_b, pair_b, sum_b, arrived_b, sems_b,
    kept_q, q0, q1, q2, q3, qsems,
    kept_k, k0, k1, k2, k3, ksems,
    kept_o, o0, o1, o2, o3, osems,
):
    ctx, me = lax.axis_index("ctx"), lax.axis_index("tp")
    rows = x_ref.shape[0]
    block, width = mixed_ref.shape
    heads = width // DH
    chip, core = ctx // 2, lax.rem(ctx, 2)
    w_load = pltpu.make_async_copy(w_hbm, w_ref, load.at[0])
    wo_load = pltpu.make_async_copy(wo_hbm, wo_ref, load.at[1])
    w_load.start()
    wo_load.start()
    others = [ctx + 1 - 2 * core]
    others += [2 * lax.rem(chip + j, chips) + core for j in range(1, chips)]
    line_barrier(ctx, me, n, others)
    gather_x = LineGather(ctx, me, n, x_ref, held_x, xsend, xrecv)
    gather_c = LineGather(ctx, me, n, cot_ref, held_c, csend, crecv)
    forward = StateSum(ctx, me, chips, False, local_f, mine_f, pair_f, sum_f, arrived_f, sems_f)
    backward = StateSum(ctx, me, chips, True, local_b, mine_b, pair_b, sum_b, arrived_b, sems_b)
    reduce_o = SlabReduce(
        ctx, me, chips, factor, held_c, mixed_ref, 0, kept_o, (o0, o1, o2, o3), osems
    )
    reduce_q = SlabReduce(
        ctx, me, chips, factor, normed_ref, gproj_ref, 0, kept_q, (q0, q1, q2, q3), qsems
    )
    reduce_k = SlabReduce(
        ctx, me, chips, factor, normed_ref, gproj_ref, width, kept_k, (k0, k1, k2, k3), ksems
    )

    def row_at(origin):
        return pl.ds(pl.multiple_of(origin * rows, rows), rows)

    def cols(h, part=0):
        return pl.ds(pl.multiple_of(part * width + h * DH, DH), DH)

    def head_rows(h):
        return pl.ds(pl.multiple_of(h * DH, DH), DH)

    def causal(value):
        down = lax.broadcasted_iota(jnp.int32, (block, block), 0)
        across = lax.broadcasted_iota(jnp.int32, (block, block), 1)
        return jnp.where(down >= across, value, 0.0).astype(BF16)

    def cotangent_turn(d):
        @pl.when(me == d)
        def _():
            gather_c.start_up()

        @pl.when(me == n - 1 - d)
        def _():
            gather_c.start_down()

    def project(source, origin):
        at = row_at(origin)
        piece = source[...].astype(F32)
        normed_ref[at, :] = (piece * row_scale(piece) * in_gain_ref[...]).astype(BF16)
        for part in range(3):
            here = slice(part * width, (part + 1) * width)
            proj_ref[at, here] = dot(normed_ref[at, :], w_ref[part]).astype(BF16)

    gather_x.start_up()
    gather_x.start_down()
    cotangent_turn(0)
    held_c[row_at(me), :] = cot_ref[...]
    w_load.wait()
    project(x_ref, me)

    @pl.loop(1, n)
    def _(d):
        gather_x.step(d)
        cotangent_turn(d)

        @pl.when(me - d >= 0)
        def _():
            project(gather_x.at(me - d), me - d)

        @pl.when(me + d < n)
        def _():
            project(gather_x.at(me + d), me + d)

    @pl.loop(0, heads)
    def _(h):
        local_f[head_rows(h), :] = dot(proj_ref[:, cols(h, 1)], proj_ref[:, cols(h, 2)], TN)

    forward.start()

    @pl.loop(0, heads)
    def _(h):
        scores[h] = causal(dot(proj_ref[:, cols(h)], proj_ref[:, cols(h, 1)], NT))

    forward.spread()
    gather_c.step(1)

    @pl.loop(0, heads)
    def _(h):
        attended[:, cols(h)] = dot(scores[h], proj_ref[:, cols(h, 2)])

    forward.collect()

    @pl.loop(0, heads)
    def _(h):
        high, low = split(local_f[head_rows(h), :])
        query = proj_ref[:, cols(h)]
        value = attended[:, cols(h)] + dot(query, high) + dot(query, low)
        attended[:, cols(h)] = value
        mixed_ref[:, cols(h)] = (value * row_scale(value) * gain_ref[:, cols(h)]).astype(BF16)

    wo_load.wait()

    def out_partial(t, into):
        @pl.loop(0, wo_ref.shape[1] // 512)
        def _(tile):
            columns = pl.ds(pl.multiple_of(tile * 512, 512), 512)
            into[:, columns] = dot(mixed_ref[row_at(t), :], wo_ref[:, columns])

    scatter = LineScatter(ctx, me, n, out_partial, total, out_a, up_a, down_a, asend, arecv)
    scatter.step(0)

    def grad_rows(origin):
        at = row_at(origin)
        weighted = dot(held_c[at, :], wo_ref[...], NT) * gain_ref[...]
        for h in range(heads):
            here = slice(h * DH, (h + 1) * DH)
            value = attended[at, here]
            scale = row_scale(value)
            part = weighted[:, here]
            mean = jnp.mean(part * value, axis=-1, keepdims=True)
            gatt[at, here] = (scale * part - scale * scale * scale * value * mean).astype(BF16)

    def grad_pair(d):
        @pl.when(me - d >= 0)
        def _():
            grad_rows(me - d)

        @pl.when(me + d < n)
        def _():
            grad_rows(me + d)

    gather_c.step(2)
    grad_rows(me)

    @pl.loop(1, n - 1)
    def _(d):
        grad_pair(d)

    scatter.step(1)
    for d in range(3, n):
        gather_c.step(d)
        grad_pair(d)

    @pl.loop(0, heads)
    def _(h):
        local_b[head_rows(h), :] = dot(proj_ref[:, cols(h)], gatt[:, cols(h)], TN)

    backward.start()

    @pl.loop(0, heads)
    def _(h):
        query, key = proj_ref[:, cols(h)], proj_ref[:, cols(h, 1)]
        grad = gatt[:, cols(h)]
        gscores = causal(dot(grad, proj_ref[:, cols(h, 2)], NT))
        high, low = split(local_f[head_rows(h), :])
        gquery = dot(gscores, key) + dot(grad, high, NT) + dot(grad, low, NT)
        gproj_ref[:, cols(h)] = gquery.astype(BF16)
        gkey[:, cols(h)] = dot(gscores, query, TN)

        @pl.when(h == 0)
        def _():
            backward.spread()

    @pl.loop(0, heads)
    def _(h):
        attended[:, cols(h)] = dot(scores[h], gatt[:, cols(h)], TN)

    for s in range(2, n - 1):
        scatter.step(s)
    run_slabs([reduce_o, reduce_q])
    backward.collect()

    @pl.loop(0, heads)
    def _(h):
        high, low = split(local_b[head_rows(h), :])
        key, value = proj_ref[:, cols(h, 1)], proj_ref[:, cols(h, 2)]
        gk = gkey[:, cols(h)] + dot(value, high, NT) + dot(value, low, NT)
        gv = attended[:, cols(h)] + dot(key, high) + dot(key, low)
        gproj_ref[:, cols(h, 1)] = gk.astype(BF16)
        gproj_ref[:, cols(h, 2)] = gv.astype(BF16)

    def in_partial(t, into):
        at = row_at(t)

        @pl.loop(0, w_ref.shape[1] // 512)
        def _(tile):
            columns = pl.ds(pl.multiple_of(tile * 512, 512), 512)
            value = dot(gproj_ref[at, :width], w_ref[0, columns, :], NT)
            for part in range(1, 3):
                here = slice(part * width, (part + 1) * width)
                value += dot(gproj_ref[at, here], w_ref[part, columns, :], NT)
            into[:, columns] = value

    back = LineScatter(ctx, me, n, in_partial, total, out_g, up_g, down_g, gsend, grecv)
    back.step(0)

    def between(j):
        @pl.when(j == chips)
        def _():
            back.step(1)

    run_slabs([reduce_k], between)
    reduce_k.keep_own()
    scatter.finish()
    outputs_ref[...] = total[...]
    for s in range(2, n - 1):
        back.step(s)
    reduce_o.keep_own()
    reduce_q.keep_own()
    reduce_o.collect()
    ograd_ref[...] = kept_o[...]
    reduce_q.collect()
    qgrad_ref[0] = kept_q[...]
    reduce_k.collect(1, chips - 1)
    back.finish()
    piece = x_ref[...].astype(F32)
    scale = row_scale(piece)
    weighted = total[...] * in_gain_ref[...]
    mean = jnp.mean(weighted * piece, axis=-1, keepdims=True)
    igrad_ref[...] = (
        cot_ref[...].astype(F32) + scale * weighted - scale * scale * scale * piece * mean
    ).astype(BF16)
    reduce_k.collect(chips - 1)
    for part in range(2):
        qgrad_ref[part + 1] = kept_k[:, part * width : (part + 1) * width]
    gather_x.finish()
    gather_c.finish()
    reduce_o.finish()
    reduce_q.finish()
    reduce_k.finish()


def vmem(*shape, dtype=BF16):
    return pltpu.VMEM(shape, dtype)


def shards(inputs, norm_gain, qkv_weight, head_gain, out_weight, out_cotangent):
    rows, width = inputs.shape
    local_width = qkv_weight.shape[2]
    heads = local_width // DH
    n = lax.axis_size("tp")
    ctx_size = lax.axis_size("ctx")
    chips = ctx_size // 2
    block = rows * n
    slab = width // ctx_size
    factor = 1.0 / math.sqrt(block * ctx_size)
    dma = pltpu.SemaphoreType.DMA
    shape = jax.ShapeDtypeStruct
    gather = [vmem(block, width), dma((2, n)), dma((n,))]
    line = [vmem(n, rows, width)] * 3 + [dma((n,)), dma((2, n))]
    state = [
        vmem(heads * DH, DH, dtype=F32),
        vmem(heads * DH, DH),
        vmem(heads * DH, DH),
        vmem(heads * DH, DH),
        vmem(chips, heads * DH, DH),
        dma((2, chips + 1)),
    ]

    def slabs(columns):
        return [vmem(slab, columns, dtype=F32)] + [vmem(chips, slab, columns)] * 4 + [
            dma((4, chips))
        ]

    scratch = (
        [vmem(3, width, local_width), vmem(local_width, width), dma((2,))]
        + [vmem(block, width), vmem(block, 3 * local_width)]
        + [vmem(block, local_width), vmem(block, 3 * local_width)]
        + gather
        + gather
        + [vmem(rows, width, dtype=F32)]
        + line
        + line
        + [vmem(heads, block, block), vmem(block, local_width, dtype=F32)]
        + [vmem(block, local_width), vmem(block, local_width, dtype=F32)]
        + state
        + state
        + slabs(local_width)
        + slabs(2 * local_width)
        + slabs(local_width)
    )
    held = pl.BlockSpec(memory_space=pltpu.VMEM)
    anywhere = pl.BlockSpec(memory_space=pl.ANY)
    summed, input_grad, qkv_grad, out_grad_t = pl.pallas_call(
        functools.partial(block_kernel, n, chips, factor),
        name="block",
        out_shape=[
            shape((rows, width), F32),
            shape((rows, width), BF16),
            shape((3, slab, local_width), F32),
            shape((slab, local_width), F32),
        ],
        in_specs=[held] * 4 + [anywhere] * 2,
        out_specs=[held] * 4,
        scratch_shapes=scratch,
        compiler_params=pltpu.CompilerParams(
            collective_id=0, has_side_effects=True, vmem_limit_bytes=VMEM_LIMIT
        ),
    )(
        inputs,
        out_cotangent,
        norm_gain.reshape(1, width),
        head_gain.reshape(1, local_width),
        qkv_weight.transpose(1, 0, 2),
        out_weight,
    )
    outputs = (inputs.astype(F32) + summed).astype(BF16)
    return (outputs, input_grad, qkv_grad.transpose(1, 0, 2), out_grad_t)


def solution(mesh):
    in_specs = (
        P(("ctx", "tp"), None),
        P(),
        P(None, None, "tp"),
        P("tp"),
        P("tp", None),
        P(("ctx", "tp"), None),
    )
    out_specs = (
        P(("ctx", "tp"), None),
        P(("ctx", "tp"), None),
        P("ctx", None, "tp"),
        P("ctx", "tp"),
    )
    return jax.shard_map(shards, mesh=mesh, in_specs=in_specs, out_specs=out_specs, check_vma=False)
```
